256 devices in a mesh: occ: 16 (over z, x_lo), aux: 16 (over x_hi, y, core).
Axes of the slice: x: 4 (x_hi: 2, x_lo: 2; x = x_hi * 2 + x_lo), y: 4, z: 8, core: 2. Of those that a mesh axis runs over, the one named last changes fastest.
Arguments:
- three_index: bfloat16 [16, 448, 6144], P('occ', None, 'aux'), may hold values from -0.75 to 0.75
- occ_energy: float32 [16], P('occ'), may hold values from -2 to -0.3
- vir_energy: float32 [448], replicated, may hold values from 0.3 to 3
Outputs:
- gamma: float32 [16, 448, 6144], P('occ', None, 'aux')
The draws below stay inside these ranges and needn't reach their ends.
All inputs are finite; a program needn't handle non-finite values.
Results may differ from the reference program's by a relative error of at most 0.0019.
Values may be sent and summed in bfloat16 or wider, within the bound.
No kernel may reach another device: no remote copies, remote signals or barrier semaphores. Data moves between devices by JAX's collectives and lax.ppermute only.
A program may use at most 64 MiB of HBM per device.

```python
import jax
import jax.numpy as jnp
from jax import lax

NVIR = 448
NOCC = 16
NAUX = 6144


def steps_of(rng, extent, cuts, least, top_value):
    level = 1.0
    for axis_at, parts in cuts:
        steps = jax.random.uniform(jax.random.fold_in(jax.random.fold_in(rng, 6), axis_at), (parts,), jnp.float32, least / len(cuts), top_value / len(cuts))
        level = level * jnp.repeat(jnp.exp(steps), extent[axis_at] // parts).reshape((-1,) + (1,) * (len(extent) - 1 - axis_at))
    return level


def noise(stream_key, dims, deviation, most, pieces=(), kind=jnp.bfloat16):
    result = deviation * jax.random.normal(stream_key, dims, jnp.float32)
    if pieces:
        result = result * steps_of(stream_key, dims, pieces, -0.22, 0.18)
    return jnp.clip(result, -most, most).astype(kind)


def setup_inputs(seed: int = 0) -> dict:
    key_of = jax.random.split(jax.random.key(seed), 4)
    return {
        "three_index": noise(key_of[0], (NOCC, NVIR, NAUX), 0.05, 0.75, ((0, 16), (2, 16))),
        "occ_energy": jnp.clip(-2.0 + 1.7 * jax.random.uniform(key_of[1], (NOCC,), jnp.float32) ** steps_of(key_of[1], (NOCC,), ((0, 16),), -0.2, 0.2), -2.0, -0.3),
        "vir_energy": jnp.clip(jax.random.uniform(key_of[2], (NVIR,), jnp.float32, 0.3, 3.0), 0.3, 3.0),
    }


def reference(three_index, occ_energy, vir_energy):
    rows = three_index.reshape(NOCC * NVIR, NAUX)
    pair = lax.dot_general(rows, rows, (((1,), (1,)), ((), ())), preferred_element_type=jnp.float32)
    four = pair.reshape(NOCC, NVIR, NOCC, NVIR)
    swapped = jnp.transpose(four, (0, 3, 2, 1))
    denom = (vir_energy[None, :, None, None] + vir_energy[None, None, None, :]
             - occ_energy[:, None, None, None] - occ_energy[None, None, :, None])
    amps = ((2.0 * four - swapped) / denom).astype(jnp.bfloat16).reshape(NOCC * NVIR, NOCC * NVIR)
    gamma = jnp.dot(amps, rows, preferred_element_type=jnp.float32)
    return gamma.reshape(NOCC, NVIR, NAUX)
```

```python
import jax
import jax.numpy as jnp
from jax import lax
from jax.sharding import Mesh, PartitionSpec as P

NZ, NXL, NXH, NY, NC = 8, 2, 2, 4, 2
ALL = ("z", "xl", "xh", "y", "c")


def flat(z, xl, xh, y, c):
    return (((z % NZ * NXL + xl % NXL) * NXH + xh % NXH) * NY + y % NY) * NC + c % NC


def moved(array, where):
    pairs = [
        (flat(z, xl, xh, y, c), flat(*where(z, xl, xh, y, c)))
        for z in range(NZ)
        for xl in range(NXL)
        for xh in range(NXH)
        for y in range(NY)
        for c in range(NC)
    ]
    return lax.ppermute(array, ALL, pairs)


def dot_nt(a, b):
    return lax.dot_general(a, b, (((1,), (1,)), ((), ())), preferred_element_type=jnp.float32)


def dot_tn(a, b):
    return lax.dot_general(a, b, (((0,), (0,)), ((), ())), preferred_element_type=jnp.float32)


def local(three_index, occ_energy, vir_energy):
    own = three_index[0]
    nvir, depth = own.shape
    group = NXH * NY
    share = nvir // group
    z, xl, c = lax.axis_index("z"), lax.axis_index("xl"), lax.axis_index("c")
    member = lax.axis_index("xh") * NY + lax.axis_index("y")

    energies = lax.all_gather(occ_energy, ("z", "xl"), axis=0, tiled=True)
    other = moved(own, lambda z, xl, xh, y, c: (z, xl, xh, y, 1 - c))
    mine = jnp.concatenate([own, other], axis=1)
    start = moved(mine, lambda z, xl, xh, y, c: (z, xl if c == 0 else 1 - xl, xh, y, c))

    ahead = [start]
    for _ in range(4):
        ahead.append(moved(ahead[-1], lambda z, xl, xh, y, c: (z - 1 if c == 0 else z + 1, xl, xh, y, c)))
    behind = [start]
    for _ in range(3):
        behind.append(moved(behind[-1], lambda z, xl, xh, y, c: (z + 1 if c == 0 else z - 1, xl, xh, y, c)))

    double = mine * jnp.bfloat16(2)
    numer = jnp.stack([dot_nt(double, block) - dot_nt(block, mine) for block in ahead])
    parts = numer.reshape(5, group, share, nvir).transpose(1, 0, 2, 3)
    parts = lax.all_to_all(parts, ("xh", "y"), 0, 0, tiled=True)
    numer = jnp.sum(parts, axis=0)

    vir_rows = lax.dynamic_slice_in_dim(vir_energy, member * share, share)
    amps = []
    for d in range(5):
        zj = jnp.where(c == 0, z + d, z - d + NZ) % NZ
        xj = jnp.where(c == 0, xl, 1 - xl)
        eps_j = lax.dynamic_slice_in_dim(energies, zj * NXL + xj, 1)
        denom = vir_rows[:, None] + vir_energy[None, :] - occ_energy[0] - eps_j[0]
        amps.append((numer[d] / denom).astype(jnp.bfloat16))
    for d in range(1, 4):
        amps.append(
            moved(
                amps[d],
                lambda z, xl, xh, y, c: (z + d, xl, xh, y, c) if c == 0 else (z - d, 1 - xl, xh, y, c),
            )
        )
    rows = jnp.stack(amps)
    copies = jnp.broadcast_to(rows, (group, *rows.shape))
    gathered = lax.all_to_all(copies, ("xh", "y"), 0, 0, tiled=True)
    gathered = gathered.transpose(1, 0, 2, 3).reshape(8, nvir, nvir)

    total = jnp.zeros((nvir, 2 * depth), jnp.float32)
    for d in range(5):
        total = total + jnp.dot(gathered[d], ahead[d], preferred_element_type=jnp.float32)
    for d in range(1, 4):
        total = total + dot_tn(gathered[4 + d], behind[d])
    back = moved(total[:, depth:], lambda z, xl, xh, y, c: (z, xl, xh, y, 1 - c))
    return (total[:, :depth] + back)[None]


def solution(mesh):
    grid = Mesh(mesh.devices.reshape(NZ, NXL, NXH, NY, NC), ALL)
    return jax.shard_map(
        local,
        mesh=grid,
        in_specs=(P(("z", "xl"), None, ("xh", "y", "c")), P(("z", "xl")), P()),
        out_specs=P(("z", "xl"), None, ("xh", "y", "c")),
        check_vma=False,
    )
```

```python
import jax
import jax.numpy as jnp
from jax import lax
from jax.sharding import Mesh, PartitionSpec as P

NZ, NXL, NXH, NY, NC = 8, 2, 2, 4, 2
ALL = ("z", "xl", "xh", "y", "c")
CHUNKS = ((0, 1), (2, 3), (4,))


def flat(z, xl, xh, y, c):
    return (((z % NZ * NXL + xl % NXL) * NXH + xh % NXH) * NY + y % NY) * NC + c % NC


def moved(array, where):
    pairs = [
        (flat(z, xl, xh, y, c), flat(*where(z, xl, xh, y, c)))
        for z in range(NZ)
        for xl in range(NXL)
        for xh in range(NXH)
        for y in range(NY)
        for c in range(NC)
    ]
    return lax.ppermute(array, ALL, pairs)


def dot_nt(a, b):
    return lax.dot_general(a, b, (((1,), (1,)), ((), ())), preferred_element_type=jnp.float32)


def dot_tn(a, b):
    return lax.dot_general(a, b, (((0,), (0,)), ((), ())), preferred_element_type=jnp.float32)


def local(three_index, occ_energy, vir_energy):
    own = three_index[0]
    nvir, depth = own.shape
    group = NXH * NY
    share = nvir // group
    z, xl, c = lax.axis_index("z"), lax.axis_index("xl"), lax.axis_index("c")
    member = lax.axis_index("xh") * NY + lax.axis_index("y")

    copies = jnp.broadcast_to(occ_energy, (NZ * NXL, 1))
    energies = lax.all_to_all(copies, ("z", "xl"), 0, 0, tiled=True)[:, 0]
    other = moved(own, lambda z, xl, xh, y, c: (z, xl, xh, y, 1 - c))
    mine = jnp.concatenate([own, other], axis=1)
    start = moved(mine, lambda z, xl, xh, y, c: (z, xl if c == 0 else 1 - xl, xh, y, c))

    ahead = [start]
    for _ in range(4):
        ahead.append(moved(ahead[-1], lambda z, xl, xh, y, c: (z - 1 if c == 0 else z + 1, xl, xh, y, c)))
    behind = [start]
    for _ in range(3):
        behind.append(moved(behind[-1], lambda z, xl, xh, y, c: (z + 1 if c == 0 else z - 1, xl, xh, y, c)))

    ahead[1], energies = lax.optimization_barrier((ahead[1], energies))

    double = mine * jnp.bfloat16(2)
    vir_rows = lax.dynamic_slice_in_dim(vir_energy, member * share, share)

    def summed(steps):
        numer = [dot_nt(double, ahead[d]) - dot_nt(ahead[d], mine) for d in steps]
        parts = jnp.stack([part.reshape(group, share, nvir) for part in numer], axis=1)
        return jnp.sum(lax.all_to_all(parts, ("xh", "y"), 0, 0, tiled=True), axis=0)

    def amps_of(d, numer):
        zj = jnp.where(c == 0, z + d, z - d + NZ) % NZ
        xj = jnp.where(c == 0, xl, 1 - xl)
        eps_j = lax.dynamic_slice_in_dim(energies, zj * NXL + xj, 1)
        denom = vir_rows[:, None] + vir_energy[None, :] - occ_energy[0] - eps_j[0]
        return (numer / denom).astype(jnp.bfloat16)

    def mirrored(d, amps):
        return moved(
            amps,
            lambda z, xl, xh, y, c: (z + d, xl, xh, y, c) if c == 0 else (z - d, 1 - xl, xh, y, c),
        )

    def gathered(parts):
        rows = jnp.stack(parts)
        copies = jnp.broadcast_to(rows, (group, *rows.shape))
        whole = lax.all_to_all(copies, ("xh", "y"), 0, 0, tiled=True)
        return [whole[:, n].reshape(nvir, nvir) for n in range(len(parts))]

    total = jnp.zeros((nvir, 2 * depth), jnp.float32)
    for steps in CHUNKS:
        numer = summed(steps)
        amps = [amps_of(d, numer[n]) for n, d in enumerate(steps)]
        turned = [d for d in steps if 0 < d < 4]
        blocks = gathered(amps + [mirrored(d, amps[steps.index(d)]) for d in turned])
        for n, d in enumerate(steps):
            total = total + jnp.dot(blocks[n], ahead[d], preferred_element_type=jnp.float32)
        for n, d in enumerate(turned):
            total = total + dot_tn(blocks[len(steps) + n], behind[d])
    back = moved(total[:, depth:], lambda z, xl, xh, y, c: (z, xl, xh, y, 1 - c))
    return (total[:, :depth] + back)[None]


def solution(mesh):
    grid = Mesh(mesh.devices.reshape(NZ, NXL, NXH, NY, NC), ALL)
    return jax.shard_map(
        local,
        mesh=grid,
        in_specs=(P(("z", "xl"), None, ("xh", "y", "c")), P(("z", "xl")), P()),
        out_specs=P(("z", "xl"), None, ("xh", "y", "c")),
        check_vma=False,
    )
```

```python
import jax
import jax.numpy as jnp
from jax import lax
from jax.sharding import Mesh, PartitionSpec as P

NZ, NXL, NXH, NY, NC = 8, 2, 2, 4, 2
ALL = ("z", "xl", "xh", "y", "c")


def flat(z, xl, xh, y, c):
    return (((z % NZ * NXL + xl % NXL) * NXH + xh % NXH) * NY + y % NY) * NC + c % NC


def moved(array, where):
    pairs = [
        (flat(z, xl, xh, y, c), flat(*where(z, xl, xh, y, c)))
        for z in range(NZ)
        for xl in range(NXL)
        for xh in range(NXH)
        for y in range(NY)
        for c in range(NC)
    ]
    return lax.ppermute(array, ALL, pairs)


def across(array):
    return moved(array, lambda z, xl, xh, y, c: (z, xl, 1 - xh, y, c))


def dot_nt(a, b):
    return lax.dot_general(a, b, (((1,), (1,)), ((), ())), preferred_element_type=jnp.float32)


def dot_tn(a, b):
    return lax.dot_general(a, b, (((0,), (0,)), ((), ())), preferred_element_type=jnp.float32)


def half_of(array, which, dim):
    return lax.dynamic_index_in_dim(array, which, dim, keepdims=False)


def local(three_index, occ_energy, vir_energy):
    own = three_index[0]
    nvir, depth = own.shape
    share = nvir // (NXH * NY)
    z, xl, c = lax.axis_index("z"), lax.axis_index("xl"), lax.axis_index("c")
    xh, y = lax.axis_index("xh"), lax.axis_index("y")

    other = moved(own, lambda z, xl, xh, y, c: (z, xl, xh, y, 1 - c))
    mine = jnp.concatenate([own, other], axis=1)

    ahead = [moved(mine, lambda z, xl, xh, y, c: (z, xl if c == 0 else 1 - xl, xh, y, c))]
    ahead.append(moved(mine, lambda z, xl, xh, y, c: (z - 1, xl if c == 0 else 1 - xl, xh, y, c)))
    behind = [mine, moved(mine, lambda z, xl, xh, y, c: (z + 1, xl, xh, y, c))]
    copies = jnp.broadcast_to(occ_energy, (NZ * NXL, 1))
    energies = lax.all_to_all(copies, ("z", "xl"), 0, 0, tiled=True)[:, 0]
    ahead.append(moved(ahead[1], lambda z, xl, xh, y, c: (z - 1, xl, xh, y, c)))
    behind.append(moved(behind[1], lambda z, xl, xh, y, c: (z + 1, xl, xh, y, c)))
    ahead[2], behind[2], energies = lax.optimization_barrier((ahead[2], behind[2], energies))

    def numer(i, j):
        a, b = behind[i], ahead[j]
        return dot_nt(a * jnp.bfloat16(2), b) - dot_nt(b, a)

    early = jnp.stack([numer(0, 0), numer(0, 1)]).reshape(2, NXH, NY, share, nvir)
    got = across(half_of(early, 1 - xh, 1))
    early = half_of(early, xh, 1) + got
    early = early.transpose(1, 0, 2, 3).reshape(NY, 2 * share, nvir)
    late = jnp.stack([numer(0, 2), numer(1, 2), numer(2, 2)]).reshape(3, NXH, NY, share, nvir)
    late = late.transpose(2, 0, 1, 3, 4).reshape(NY, 3 * NXH * share, nvir)
    parts = jnp.concatenate([early, late], axis=1)
    sums = jnp.sum(lax.all_to_all(parts, "y", 0, 0, tiled=True), axis=0)
    early = sums[: 2 * share].reshape(2, share, nvir)
    late = sums[2 * share :].reshape(3, NXH, share, nvir)
    late = half_of(late, xh, 1) + across(half_of(late, 1 - xh, 1))

    for _ in range(2):
        ahead.append(moved(ahead[-1], lambda z, xl, xh, y, c: (z - 1, xl, xh, y, c)))
    turned = [ahead[0]]
    for _ in range(3):
        turned.append(moved(turned[-1], lambda z, xl, xh, y, c: (z + 1, xl, xh, y, c)))

    vir_rows = lax.dynamic_slice_in_dim(vir_energy, (xh * NY + y) * share, share)
    virs = vir_rows[:, None] + vir_energy[None, :]
    xc = jnp.where(c == 0, xl, 1 - xl)

    def amps(value, i, j):
        eps_i = lax.dynamic_slice_in_dim(energies, (z - i + NZ) % NZ * NXL + xl, 1)
        eps_j = lax.dynamic_slice_in_dim(energies, (z + j) % NZ * NXL + xc, 1)
        return (value / (virs - eps_i[0] - eps_j[0])).astype(jnp.bfloat16)

    p0, p1 = amps(early[0], 0, 0), amps(early[1], 0, 1)
    p2, p3, p4 = amps(late[0], 0, 2), amps(late[1], 1, 2), amps(late[2], 2, 2)

    t1 = moved(p1, lambda z, xl, xh, y, c: (z + 1, xl if c == 0 else 1 - xl, xh, y, c))
    t23 = moved(jnp.stack([p2, p3]), lambda z, xl, xh, y, c: (z + 2, xl if c == 0 else 1 - xl, xh, y, c))
    d3 = moved(p3, lambda z, xl, xh, y, c: (z - 1, xl, xh, y, c))
    d4 = moved(p4, lambda z, xl, xh, y, c: (z - 2, xl, xh, y, c))

    rows = jnp.stack([p0, p1, p2])
    rows = lax.all_to_all(jnp.broadcast_to(rows, (NY, *rows.shape)), "y", 0, 0, tiled=True)
    rows_other = across(rows)
    more = jnp.stack([d3, d4, t1, t23[0], t23[1]])
    more_other = across(more)

    def in_order(here, there):
        return jnp.where(xh == 0, jnp.stack([here, there]), jnp.stack([there, here]))

    rows = in_order(rows, rows_other).transpose(2, 0, 1, 3, 4).reshape(3, nvir, nvir)
    more = in_order(more, more_other)
    more = lax.all_to_all(jnp.broadcast_to(more, (NY, *more.shape)), "y", 0, 0, tiled=True)
    more = more.transpose(2, 1, 0, 3, 4).reshape(5, nvir, nvir)

    total = jnp.dot(rows[0], ahead[0], preferred_element_type=jnp.float32)
    for n, block in enumerate((ahead[1], ahead[2])):
        total = total + jnp.dot(rows[n + 1], block, preferred_element_type=jnp.float32)
    for n, block in enumerate((ahead[3], ahead[4])):
        total = total + jnp.dot(more[n], block, preferred_element_type=jnp.float32)
    for n in range(3):
        total = total + dot_tn(more[2 + n], turned[n + 1])
    back = moved(total[:, depth:], lambda z, xl, xh, y, c: (z, xl, xh, y, 1 - c))
    return (total[:, :depth] + back)[None]


def solution(mesh):
    grid = Mesh(mesh.devices.reshape(NZ, NXL, NXH, NY, NC), ALL)
    return jax.shard_map(
        local,
        mesh=grid,
        in_specs=(P(("z", "xl"), None, ("xh", "y", "c")), P(("z", "xl")), P()),
        out_specs=P(("z", "xl"), None, ("xh", "y", "c")),
        check_vma=False,
    )
```

```python
import jax
import jax.numpy as jnp
from jax import lax
from jax.sharding import Mesh, PartitionSpec as P

NZ, NXL, NXH, NY, NC = 8, 2, 2, 4, 2
ALL = ("z", "xl", "xh", "y", "c")


def flat(z, xl, xh, y, c):
    return (((z % NZ * NXL + xl % NXL) * NXH + xh % NXH) * NY + y % NY) * NC + c % NC


def moved(array, where):
    pairs = [
        (flat(z, xl, xh, y, c), flat(*where(z, xl, xh, y, c)))
        for z in range(NZ)
        for xl in range(NXL)
        for xh in range(NXH)
        for y in range(NY)
        for c in range(NC)
    ]
    return lax.ppermute(array, ALL, pairs)


def across(array):
    return moved(array, lambda z, xl, xh, y, c: (z, xl, 1 - xh, y, c))


def dot_nt(a, b):
    return lax.dot_general(a, b, (((1,), (1,)), ((), ())), preferred_element_type=jnp.float32)


def dot_tn(a, b):
    return lax.dot_general(a, b, (((0,), (0,)), ((), ())), preferred_element_type=jnp.float32)


def half_of(array, which, dim):
    return lax.dynamic_index_in_dim(array, which, dim, keepdims=False)


def local(three_index, occ_energy, vir_energy):
    own = three_index[0]
    nvir, depth = own.shape
    share = nvir // (NXH * NY)
    z, xl, c = lax.axis_index("z"), lax.axis_index("xl"), lax.axis_index("c")
    xh, y = lax.axis_index("xh"), lax.axis_index("y")

    other = moved(own, lambda z, xl, xh, y, c: (z, xl, xh, y, 1 - c))
    high = lax.reduce_precision(occ_energy[0], 8, 7)
    rest = occ_energy[0] - high
    middle = lax.reduce_precision(rest, 8, 7)
    column = lax.broadcasted_iota(jnp.int32, (8, 2 * depth), 1)
    tail = jnp.where(column == 0, high, jnp.where(column == 1, middle, jnp.where(column == 2, rest - middle, 0.0)))
    mine = jnp.concatenate([jnp.concatenate([own, other], axis=1), tail.astype(jnp.bfloat16)], axis=0)

    ahead = [moved(mine, lambda z, xl, xh, y, c: (z, xl if c == 0 else 1 - xl, xh, y, c))]
    ahead.append(moved(mine, lambda z, xl, xh, y, c: (z - 1, xl if c == 0 else 1 - xl, xh, y, c)))
    behind = [mine, moved(mine, lambda z, xl, xh, y, c: (z + 1, xl, xh, y, c))]
    ahead.append(moved(ahead[1], lambda z, xl, xh, y, c: (z - 1, xl, xh, y, c)))
    behind.append(moved(behind[1], lambda z, xl, xh, y, c: (z + 1, xl, xh, y, c)))

    def numer(i, j):
        a, b = behind[i][:nvir], ahead[j][:nvir]
        return dot_nt(a * jnp.bfloat16(2), b) - dot_nt(b, a)

    def halves(*values):
        value = jnp.stack(values).reshape(len(values), NXH, NY, share, nvir)
        got = across(half_of(value, 1 - xh, 1))
        value = half_of(value, xh, 1) + got
        return value.transpose(1, 0, 2, 3).reshape(NY, len(values) * share, nvir)

    def over_y(parts):
        return jnp.sum(lax.all_to_all(parts, "y", 0, 0, tiled=True), axis=0)

    def energy(block):
        terms = block[nvir, :3].astype(jnp.float32)
        return terms[0] + terms[1] + terms[2]

    vir_rows = lax.dynamic_slice_in_dim(vir_energy, (xh * NY + y) * share, share)
    virs = vir_rows[:, None] + vir_energy[None, :]

    def amps(value, i, j):
        return (value / (virs - energy(behind[i]) - energy(ahead[j]))).astype(jnp.bfloat16)

    early = halves(numer(0, 0), numer(0, 1))
    late = numer(0, 2).reshape(NXH, NY, share, nvir).transpose(1, 0, 2, 3).reshape(NY, NXH * share, nvir)
    last = halves(numer(1, 2), numer(2, 2))
    sums = over_y(jnp.concatenate([early, late], axis=1))

    for _ in range(2):
        ahead.append(moved(ahead[-1], lambda z, xl, xh, y, c: (z - 1, xl, xh, y, c)))
    turned = [ahead[0]]
    for _ in range(3):
        turned.append(moved(turned[-1], lambda z, xl, xh, y, c: (z + 1, xl, xh, y, c)))
    sums, ahead[3], turned[1] = lax.optimization_barrier((sums, ahead[3], turned[1]))

    p0, p1 = amps(sums[:share], 0, 0), amps(sums[share : 2 * share], 0, 1)
    late = sums[2 * share :].reshape(NXH, share, nvir)
    p2 = amps(half_of(late, xh, 0) + across(half_of(late, 1 - xh, 0)), 0, 2)
    t1 = moved(p1, lambda z, xl, xh, y, c: (z + 1, xl if c == 0 else 1 - xl, xh, y, c))
    t2 = moved(p2, lambda z, xl, xh, y, c: (z + 2, xl if c == 0 else 1 - xl, xh, y, c))

    last = over_y(last)
    p3, p4 = amps(last[:share], 1, 2), amps(last[share:], 2, 2)
    t3 = moved(p3, lambda z, xl, xh, y, c: (z + 2, xl if c == 0 else 1 - xl, xh, y, c))
    d3 = moved(p3, lambda z, xl, xh, y, c: (z - 1, xl, xh, y, c))
    d4 = moved(p4, lambda z, xl, xh, y, c: (z - 2, xl, xh, y, c))

    def to_all(parts):
        return lax.all_to_all(jnp.broadcast_to(parts, (NY, *parts.shape)), "y", 0, 0, tiled=True)

    def in_order(here, there):
        return jnp.where(xh == 0, jnp.stack([here, there]), jnp.stack([there, here]))

    rows = to_all(jnp.stack([p0, p1, t1]))
    rows = in_order(rows, across(rows)).transpose(2, 0, 1, 3, 4).reshape(3, nvir, nvir)
    more = jnp.stack([p2, t2, d3, d4, t3])
    more = to_all(in_order(more, across(more))).transpose(2, 1, 0, 3, 4).reshape(5, nvir, nvir)

    total = jnp.dot(rows[0], ahead[0][:nvir], preferred_element_type=jnp.float32)
    total = total + jnp.dot(rows[1], ahead[1][:nvir], preferred_element_type=jnp.float32)
    total = total + dot_tn(rows[2], turned[1][:nvir])
    for n, k in ((0, 2), (2, 3), (3, 4)):
        total = total + jnp.dot(more[n], ahead[k][:nvir], preferred_element_type=jnp.float32)
    for n, k in ((1, 2), (4, 3)):
        total = total + dot_tn(more[n], turned[k][:nvir])
    back = moved(total[:, depth:], lambda z, xl, xh, y, c: (z, xl, xh, y, 1 - c))
    return (total[:, :depth] + back)[None]


def solution(mesh):
    grid = Mesh(mesh.devices.reshape(NZ, NXL, NXH, NY, NC), ALL)
    return jax.shard_map(
        local,
        mesh=grid,
        in_specs=(P(("z", "xl"), None, ("xh", "y", "c")), P(("z", "xl")), P()),
        out_specs=P(("z", "xl"), None, ("xh", "y", "c")),
        check_vma=False,
    )
```

```python
import jax
import jax.numpy as jnp
from jax import lax
from jax.sharding import Mesh, PartitionSpec as P

NZ, NXL, NXH, NY, NC = 8, 2, 2, 4, 2
ALL = ("z", "xl", "xh", "y", "c")


def flat(z, xl, xh, y, c):
    return (((z % NZ * NXL + xl % NXL) * NXH + xh % NXH) * NY + y % NY) * NC + c % NC


def moved(array, where):
    pairs = []
    for z in range(NZ):
        for xl in range(NXL):
            for xh in range(NXH):
                for y in range(NY):
                    for c in range(NC):
                        target = where(z, xl, xh, y, c)
                        if target is not None:
                            pairs.append((flat(z, xl, xh, y, c), flat(*target)))
    return lax.ppermute(array, ALL, pairs)


def other_core(array):
    return moved(array, lambda z, xl, xh, y, c: (z, xl, xh, y, 1 - c))


def across(array):
    return moved(array, lambda z, xl, xh, y, c: (z, xl, 1 - xh, y, c))


def kind(xl, xh):
    return xl if xh == 0 else 1 - xl


def dot_nt(a, b):
    return lax.dot_general(a, b, (((1,), (1,)), ((), ())), preferred_element_type=jnp.float32)


def dot_nn(a, b):
    return lax.dot_general(a, b, (((1,), (0,)), ((), ())), preferred_element_type=jnp.float32)


def dot_tn(a, b):
    return lax.dot_general(a, b, (((0,), (0,)), ((), ())), preferred_element_type=jnp.float32)


def local(three_index, occ_energy, vir_energy):
    own = three_index[0]
    nvir, depth = own.shape
    share = nvir // NY
    c, xh, y = lax.axis_index("c"), lax.axis_index("xh"), lax.axis_index("y")

    high = lax.reduce_precision(occ_energy[0], 8, 7)
    rest = occ_energy[0] - high
    middle = lax.reduce_precision(rest, 8, 7)
    column = lax.broadcasted_iota(jnp.int32, (8, 4 * depth), 1)
    tail = jnp.where(column == 0, high, jnp.where(column == 1, middle, jnp.where(column == 2, rest - middle, 0.0)))
    there = across(own)
    beside = other_core(own)
    there_beside = other_core(there)

    def in_order(first, a, b):
        return jnp.where(first, jnp.concatenate([a, b], axis=1), jnp.concatenate([b, a], axis=1))

    mine = in_order(xh == 0, in_order(c == 0, own, beside), in_order(c == 0, there, there_beside))
    mine = jnp.concatenate([mine, tail.astype(jnp.bfloat16)], axis=0)

    step_one = moved(
        mine,
        lambda z, xl, xh, y, c: (z - 1, kind(xl, xh), xh, y, c) if c == 0 else (z + 1, xl, xh, y, c),
    )
    start, step_one = lax.optimization_barrier((mine, step_one))
    step_zero = moved(start, lambda z, xl, xh, y, c: (z, kind(xl, xh), xh, y, c) if c == 0 else None)
    step_two = moved(step_one, lambda z, xl, xh, y, c: (z - 1 if c == 0 else z + 1, xl, xh, y, c))
    swap_one = other_core(step_one)
    swap_two = moved(step_two, lambda z, xl, xh, y, c: (z, xl, xh, y, 1) if c == 0 else None)

    def numer(a, b):
        a, b = a[:nvir], b[:nvir]
        return dot_nt(a * jnp.bfloat16(2), b) - dot_nt(b, a)

    def packed(*values):
        return jnp.stack([value.reshape(NY, share, nvir) for value in values], axis=1)

    def over_y(parts):
        return jnp.sum(lax.all_to_all(parts, "y", 0, 0, tiled=True), axis=0)

    def energy(block):
        terms = block[nvir, :3].astype(jnp.float32)
        return terms[0] + terms[1] + terms[2]

    vir_rows = lax.dynamic_slice_in_dim(vir_energy, y * share, share)
    virs = vir_rows[:, None] + vir_energy[None, :]

    def amps(value, a, b):
        return (value / (virs - energy(a) - energy(b))).astype(jnp.bfloat16)

    def to_all(*parts):
        parts = jnp.stack(parts)
        whole = lax.all_to_all(jnp.broadcast_to(parts, (NY, *parts.shape)), "y", 0, 0, tiled=True)
        return [whole[:, n].reshape(nvir, nvir) for n in range(parts.shape[0])]

    rows_one = jnp.where(c == 0, mine, step_one)
    cols_one = jnp.where(c == 0, step_one, swap_one)
    parts = packed(numer(rows_one, cols_one))
    parts, swap_one = lax.optimization_barrier((parts, swap_one))
    early = over_y(parts)
    rows_two = jnp.where(c == 0, swap_one, swap_two)
    late = over_y(packed(numer(rows_two, step_two), numer(mine, step_zero)))

    turned_one = moved(step_one, lambda z, xl, xh, y, c: (z, kind(xl, xh), xh, y, 1) if c == 1 else None)
    turned_two = moved(step_two, lambda z, xl, xh, y, c: (z, kind(xl, xh), xh, y, 1) if c == 1 else None)
    step_three = moved(
        step_two,
        lambda z, xl, xh, y, c: (z - 1, xl, xh, y, c) if c == 0 else (z + 1, kind(xl, xh), xh, y, c),
    )
    turned_four = moved(step_three, lambda z, xl, xh, y, c: (z + 1, xl, xh, y, 1) if c == 1 else None)

    amps_one = amps(early[0], rows_one, cols_one)
    first = moved(
        amps_one,
        lambda z, xl, xh, y, c: (z + 1, kind(xl, xh), xh, y, 1) if c == 0 else (z - 1, xl, xh, y, 0),
    )
    second = moved(
        amps_one,
        lambda z, xl, xh, y, c: (z, xl, xh, y, 0) if c == 0 else (z + 1, kind(xl, xh), xh, y, 1),
    )
    first, second = to_all(first, second)

    amps_two = amps(late[0], rows_two, step_two)
    amps_zero = amps(late[1], mine, step_zero)
    third = moved(
        amps_two,
        lambda z, xl, xh, y, c: (z - 1, xl, xh, y, 0) if c == 0 else (z - 2, xl, xh, y, 1),
    )
    fourth = moved(amps_two, lambda z, xl, xh, y, c: (z + 2, kind(xl, xh), xh, y, 1) if c == 0 else None)
    fourth = jnp.where(c == 0, amps_zero, fourth)
    third, fourth, first, second = lax.optimization_barrier((third, fourth, first, second))
    third, fourth = to_all(third, fourth)

    def on_zero(parts, ahead, behind):
        return sum(dot_nn(part, block[:nvir]) for part, block in zip(parts, ahead))

    def on_one(parts, ahead, behind):
        return sum(dot_tn(part, block[:nvir]) for part, block in zip(parts, behind))

    total = lax.cond(c == 0, on_zero, on_one, (first, second), (step_two, step_one), (turned_one, turned_two))
    total = total + lax.cond(
        c == 0, on_zero, on_one, (third, fourth), (step_three, step_zero), (turned_four, step_three)
    )
    chunk = [total[:, n * depth : (n + 1) * depth] for n in range(NXH * NC)]
    sent = jnp.concatenate([jnp.where(c == 0, chunk[n + 1], chunk[n]) for n in (0, NC)], axis=1)
    kept = jnp.concatenate([jnp.where(c == 0, chunk[n], chunk[n + 1]) for n in (0, NC)], axis=1)
    kept = kept + other_core(sent)
    mine_now = jnp.where(xh == 0, kept[:, :depth], kept[:, depth:])
    theirs = jnp.where(xh == 0, kept[:, depth:], kept[:, :depth])
    return (mine_now + across(theirs))[None]


def solution(mesh):
    grid = Mesh(mesh.devices.reshape(NZ, NXL, NXH, NY, NC), ALL)
    return jax.shard_map(
        local,
        mesh=grid,
        in_specs=(P(("z", "xl"), None, ("xh", "y", "c")), P(("z", "xl")), P()),
        out_specs=P(("z", "xl"), None, ("xh", "y", "c")),
        check_vma=False,
    )
```

```python
import jax
import jax.numpy as jnp
from jax import lax
from jax.sharding import Mesh, PartitionSpec as P

NZ, NXL, NXH, NY, NC = 8, 2, 2, 4, 2
ALL = ("z", "xl", "xh", "y", "c")


def flat(z, xl, xh, y, c):
    return (((z % NZ * NXL + xl % NXL) * NXH + xh % NXH) * NY + y % NY) * NC + c % NC


def moved(array, where):
    pairs = []
    for z in range(NZ):
        for xl in range(NXL):
            for xh in range(NXH):
                for y in range(NY):
                    for c in range(NC):
                        target = where(z, xl, xh, y, c)
                        if target is not None:
                            pairs.append((flat(z, xl, xh, y, c), flat(*target)))
    return lax.ppermute(array, ALL, pairs)


def other_core(array):
    return moved(array, lambda z, xl, xh, y, c: (z, xl, xh, y, 1 - c))


def across(array):
    return moved(array, lambda z, xl, xh, y, c: (z, xl, 1 - xh, y, c))


def kind(xl, xh):
    return xl if xh == 0 else 1 - xl


def dot_nt(a, b):
    return lax.dot_general(a, b, (((1,), (1,)), ((), ())), preferred_element_type=jnp.float32)


def dot_nn(a, b):
    return lax.dot_general(a, b, (((1,), (0,)), ((), ())), preferred_element_type=jnp.float32)


def dot_tn(a, b):
    return lax.dot_general(a, b, (((0,), (0,)), ((), ())), preferred_element_type=jnp.float32)


def local(three_index, occ_energy, vir_energy):
    own = three_index[0]
    nvir, depth = own.shape
    share = nvir // NY
    c, xh, y = lax.axis_index("c"), lax.axis_index("xh"), lax.axis_index("y")

    high = lax.reduce_precision(occ_energy[0], 8, 7)
    rest = occ_energy[0] - high
    middle = lax.reduce_precision(rest, 8, 7)
    column = lax.broadcasted_iota(jnp.int32, (8, 4 * depth), 1)
    tail = jnp.where(column == 0, high, jnp.where(column == 1, middle, jnp.where(column == 2, rest - middle, 0.0)))
    there = across(own)
    beside = other_core(own)
    there_beside = other_core(there)

    def in_order(first, a, b):
        return jnp.where(first, jnp.concatenate([a, b], axis=1), jnp.concatenate([b, a], axis=1))

    mine = in_order(xh == 0, in_order(c == 0, own, beside), in_order(c == 0, there, there_beside))
    mine = jnp.concatenate([mine, tail.astype(jnp.bfloat16)], axis=0)

    step_one = moved(
        mine,
        lambda z, xl, xh, y, c: (z - 1, kind(xl, xh), xh, y, c) if c == 0 else (z + 1, xl, xh, y, c),
    )
    start, step_one = lax.optimization_barrier((mine, step_one))
    swap_one = other_core(step_one)
    step_two = moved(step_one, lambda z, xl, xh, y, c: (z - 1 if c == 0 else z + 1, xl, xh, y, c))
    beyond = moved(start, lambda z, xl, xh, y, c: (z, 1 - xl, xh, y, c) if (xh, c) == (1, 0) else None)
    turned_one = moved(step_one, lambda z, xl, xh, y, c: (z, 1 - xl, xh, y, c) if (xh, c) == (1, 1) else None)

    def numer(a, b):
        a, b = a[:nvir], b[:nvir]
        return dot_nt(a * jnp.bfloat16(2), b) - dot_nt(b, a)

    def packed(*values):
        return jnp.stack([value.reshape(NY, share, nvir) for value in values], axis=1)

    def over_y(parts):
        return jnp.sum(lax.all_to_all(parts, "y", 0, 0, tiled=True), axis=0)

    def energy(block):
        terms = block[nvir, :3].astype(jnp.float32)
        return terms[0] + terms[1] + terms[2]

    vir_rows = lax.dynamic_slice_in_dim(vir_energy, y * share, share)
    virs = vir_rows[:, None] + vir_energy[None, :]

    def amps(value, a, b):
        return (value / (virs - energy(a) - energy(b))).astype(jnp.bfloat16)

    def to_all(*parts):
        parts = jnp.stack(parts)
        whole = lax.all_to_all(jnp.broadcast_to(parts, (NY, *parts.shape)), "y", 0, 0, tiled=True)
        return [whole[:, n].reshape(nvir, nvir) for n in range(parts.shape[0])]

    rows_one = jnp.where(c == 0, mine, step_one)
    cols_one = jnp.where(c == 0, step_one, swap_one)
    parts = packed(numer(rows_one, cols_one))
    early = over_y(parts)
    step_two, swap_one, beyond, anchor = lax.optimization_barrier((step_two, swap_one, beyond, parts[0, 0, 0, 0]))
    swap_two = moved(step_two, lambda z, xl, xh, y, c: (z, xl, xh, y, 1) if c == 0 else None)
    step_zero = jnp.where(xh == 0, mine, beyond)
    rows_two = jnp.where(c == 0, swap_one, swap_two)
    late = over_y(packed(numer(rows_two, step_two), numer(mine, step_zero)))

    late = jnp.where(c < NC, late, anchor)

    turned_two = moved(turned_one, lambda z, xl, xh, y, c: (z + 1, xl, xh, y, c) if (xh, c) == (1, 1) else None)
    step_three = moved(
        step_two,
        lambda z, xl, xh, y, c: (z - 1, xl, xh, y, c) if c == 0 else (z + 1, kind(xl, xh), xh, y, c),
    )
    turned_four = moved(step_three, lambda z, xl, xh, y, c: (z + 1, xl, xh, y, 1) if c == 1 else None)

    amps_one = amps(early[0], rows_one, cols_one)
    first = moved(
        amps_one,
        lambda z, xl, xh, y, c: (z + 1, kind(xl, xh), xh, y, 1) if c == 0 else (z - 1, xl, xh, y, 0),
    )
    second = moved(
        amps_one,
        lambda z, xl, xh, y, c: (z + 1, kind(xl, xh), xh, y, 1) if c == 1 else None,
    )
    second = jnp.where(c == 0, amps_one, second)
    late, first, second, step_three = lax.optimization_barrier((late, first, second, step_three))
    first, second = to_all(first, second)

    amps_two = amps(late[0], rows_two, step_two)
    amps_zero = amps(late[1], mine, step_zero)
    third = moved(
        amps_two,
        lambda z, xl, xh, y, c: (z - 1, xl, xh, y, 0) if c == 0 else (z - 2, xl, xh, y, 1),
    )
    fourth = moved(amps_two, lambda z, xl, xh, y, c: (z + 2, kind(xl, xh), xh, y, 1) if c == 0 else None)
    fourth = jnp.where(c == 0, amps_zero, fourth)
    third, fourth, first, second = lax.optimization_barrier((third, fourth, first, second))
    third, fourth = to_all(third, fourth)

    def product(dot, *blocks):
        return lambda parts: sum(dot(part, block[:nvir]) for part, block in zip(parts, blocks))

    case = xh * NC + c
    total = lax.switch(
        case,
        [
            product(dot_nn, step_two, step_one),
            product(dot_tn, step_one, step_two),
            product(dot_nn, step_two, step_one),
            product(dot_tn, turned_one, turned_two),
        ],
        (first, second),
    )
    total = total + lax.switch(
        case,
        [
            product(dot_nn, step_three, mine),
            product(dot_tn, turned_four, step_three),
            product(dot_nn, step_three, beyond),
            product(dot_tn, turned_four, step_three),
        ],
        (third, fourth),
    )
    chunk = [total[:, n * depth : (n + 1) * depth] for n in range(NXH * NC)]
    sent = jnp.concatenate([jnp.where(c == 0, chunk[n + 1], chunk[n]) for n in (0, NC)], axis=1)
    kept = jnp.concatenate([jnp.where(c == 0, chunk[n], chunk[n + 1]) for n in (0, NC)], axis=1)
    kept = kept + other_core(sent)
    mine_now = jnp.where(xh == 0, kept[:, :depth], kept[:, depth:])
    theirs = jnp.where(xh == 0, kept[:, depth:], kept[:, :depth])
    return (mine_now + across(theirs))[None]


def solution(mesh):
    grid = Mesh(mesh.devices.reshape(NZ, NXL, NXH, NY, NC), ALL)
    return jax.shard_map(
        local,
        mesh=grid,
        in_specs=(P(("z", "xl"), None, ("xh", "y", "c")), P(("z", "xl")), P()),
        out_specs=P(("z", "xl"), None, ("xh", "y", "c")),
        check_vma=False,
    )
```

```python
import jax
import jax.numpy as jnp
from jax import lax
from jax.sharding import Mesh, PartitionSpec as P

NZ, NXL, NXH, NY, NC = 8, 2, 2, 4, 2
ALL = ("z", "xl", "xh", "y", "c")


def flat(z, xl, xh, y, c):
    return (((z % NZ * NXL + xl % NXL) * NXH + xh % NXH) * NY + y % NY) * NC + c % NC


def moved(array, where):
    pairs = []
    for z in range(NZ):
        for xl in range(NXL):
            for xh in range(NXH):
                for y in range(NY):
                    for c in range(NC):
                        target = where(z, xl, xh, y, c)
                        if target is not None:
                            pairs.append((flat(z, xl, xh, y, c), flat(*target)))
    return lax.ppermute(array, ALL, pairs)


def other_core(array):
    return moved(array, lambda z, xl, xh, y, c: (z, xl, xh, y, 1 - c))


def across(array):
    return moved(array, lambda z, xl, xh, y, c: (z, xl, 1 - xh, y, c))


def kind(xl, xh):
    return xl if xh == 0 else 1 - xl


def dot_nt(a, b):
    return lax.dot_general(a, b, (((1,), (1,)), ((), ())), preferred_element_type=jnp.float32)


def dot_nn(a, b):
    return lax.dot_general(a, b, (((1,), (0,)), ((), ())), preferred_element_type=jnp.float32)


def dot_tn(a, b):
    return lax.dot_general(a, b, (((0,), (0,)), ((), ())), preferred_element_type=jnp.float32)


def local(three_index, occ_energy, vir_energy):
    own = three_index[0]
    nvir, depth = own.shape
    share = nvir // NY
    c, xh, y = lax.axis_index("c"), lax.axis_index("xh"), lax.axis_index("y")

    high = lax.reduce_precision(occ_energy[0], 8, 7)
    rest = occ_energy[0] - high
    middle = lax.reduce_precision(rest, 8, 7)
    column = lax.broadcasted_iota(jnp.int32, (8, 4 * depth), 1)
    tail = jnp.where(column == 0, high, jnp.where(column == 1, middle, jnp.where(column == 2, rest - middle, 0.0)))
    there = across(own)
    beside = other_core(own)
    there_beside = other_core(there)

    def in_order(first, a, b):
        return jnp.where(first, jnp.concatenate([a, b], axis=1), jnp.concatenate([b, a], axis=1))

    mine = in_order(xh == 0, in_order(c == 0, own, beside), in_order(c == 0, there, there_beside))
    mine = jnp.concatenate([mine, tail.astype(jnp.bfloat16)], axis=0)

    step_one = moved(
        mine,
        lambda z, xl, xh, y, c: (z - 1, kind(xl, xh), xh, y, c) if c == 0 else (z + 1, xl, xh, y, c),
    )
    beyond = moved(mine, lambda z, xl, xh, y, c: (z, 1 - xl, 1, y, c) if (xh, c) == (0, 0) else None)
    swap_one = other_core(step_one)
    step_two = moved(step_one, lambda z, xl, xh, y, c: (z - 1 if c == 0 else z + 1, xl, xh, y, c))
    turned_one = moved(step_one, lambda z, xl, xh, y, c: (z, 1 - xl, 1, y, c) if (xh, c) == (0, 1) else None)

    def numer(a, b):
        a, b = a[:nvir], b[:nvir]
        return dot_nt(a * jnp.bfloat16(2), b) - dot_nt(b, a)

    def packed(*values):
        return jnp.stack([value.reshape(NY, share, nvir) for value in values], axis=1)

    def over_y(parts):
        return jnp.sum(lax.all_to_all(parts, "y", 0, 0, tiled=True), axis=0)

    def energy(block):
        terms = block[nvir, :3].astype(jnp.float32)
        return terms[0] + terms[1] + terms[2]

    vir_rows = lax.dynamic_slice_in_dim(vir_energy, y * share, share)
    virs = vir_rows[:, None] + vir_energy[None, :]

    def amps(value, a, b):
        return (value / (virs - energy(a) - energy(b))).astype(jnp.bfloat16)

    def to_all(*parts):
        parts = jnp.stack(parts)
        whole = lax.all_to_all(jnp.broadcast_to(parts, (NY, *parts.shape)), "y", 0, 0, tiled=True)
        return [whole[:, n].reshape(nvir, nvir) for n in range(parts.shape[0])]

    rows_one = jnp.where(c == 0, mine, step_one)
    cols_one = jnp.where(c == 0, step_one, swap_one)
    step_zero = jnp.where(xh == 0, mine, beyond)
    parts = lax.optimization_barrier(packed(numer(rows_one, cols_one), numer(mine, step_zero)))
    early = over_y(parts)
    step_two, swap_one, anchor = lax.optimization_barrier((step_two, swap_one, parts[0, 0, 0, 0]))
    swap_two = moved(step_two, lambda z, xl, xh, y, c: (z, xl, xh, y, 1) if c == 0 else None)
    rows_two = jnp.where(c == 0, swap_one, swap_two)
    late = over_y(packed(numer(rows_two, step_two)))
    late = jnp.where(c < NC, late, anchor)

    turned_two = moved(turned_one, lambda z, xl, xh, y, c: (z + 1, xl, xh, y, c) if (xh, c) == (1, 1) else None)
    step_three = moved(
        step_two,
        lambda z, xl, xh, y, c: (z - 1, xl, xh, y, c) if c == 0 else (z + 1, kind(xl, xh), xh, y, c),
    )
    turned_four = moved(step_three, lambda z, xl, xh, y, c: (z + 1, xl, xh, y, 1) if c == 1 else None)

    amps_one = amps(early[0], rows_one, cols_one)
    amps_zero = amps(early[1], mine, step_zero)
    first = moved(
        amps_one,
        lambda z, xl, xh, y, c: (z + 1, kind(xl, xh), xh, y, 1) if c == 0 else (z - 1, xl, xh, y, 0),
    )
    second = moved(
        amps_one,
        lambda z, xl, xh, y, c: (z + 1, kind(xl, xh), xh, y, 1) if c == 1 else None,
    )
    second = jnp.where(c == 0, amps_one, second)
    late, first, second, step_three, amps_zero = lax.optimization_barrier((late, first, second, step_three, amps_zero))
    first, second = to_all(first, second)

    amps_two = amps(late[0], rows_two, step_two)
    third = moved(
        amps_two,
        lambda z, xl, xh, y, c: (z - 1, xl, xh, y, 0) if c == 0 else (z - 2, xl, xh, y, 1),
    )
    fourth = moved(amps_two, lambda z, xl, xh, y, c: (z + 2, kind(xl, xh), xh, y, 1) if c == 0 else None)
    fourth = jnp.where(c == 0, amps_zero, fourth)
    third, fourth, first, second = lax.optimization_barrier((third, fourth, first, second))
    third, fourth = to_all(third, fourth)

    def product(dot, *blocks):
        return lambda parts: sum(dot(part, block[:nvir]) for part, block in zip(parts, blocks))

    case = xh * NC + c
    total = lax.switch(
        case,
        [
            product(dot_nn, step_two, step_one),
            product(dot_tn, step_one, step_two),
            product(dot_nn, step_two, step_one),
            product(dot_tn, turned_one, turned_two),
        ],
        (first, second),
    )
    total = total + lax.switch(
        case,
        [
            product(dot_nn, step_three, mine),
            product(dot_tn, turned_four, step_three),
            product(dot_nn, step_three, beyond),
            product(dot_tn, turned_four, step_three),
        ],
        (third, fourth),
    )
    chunk = [total[:, n * depth : (n + 1) * depth] for n in range(NXH * NC)]
    sent = jnp.concatenate([jnp.where(c == 0, chunk[n + 1], chunk[n]) for n in (0, NC)], axis=1)
    kept = jnp.concatenate([jnp.where(c == 0, chunk[n], chunk[n + 1]) for n in (0, NC)], axis=1)
    kept = kept + other_core(sent)
    mine_now = jnp.where(xh == 0, kept[:, :depth], kept[:, depth:])
    theirs = jnp.where(xh == 0, kept[:, depth:], kept[:, :depth])
    return (mine_now + across(theirs))[None]


def solution(mesh):
    grid = Mesh(mesh.devices.reshape(NZ, NXL, NXH, NY, NC), ALL)
    return jax.shard_map(
        local,
        mesh=grid,
        in_specs=(P(("z", "xl"), None, ("xh", "y", "c")), P(("z", "xl")), P()),
        out_specs=P(("z", "xl"), None, ("xh", "y", "c")),
        check_vma=False,
    )
```

```python
import jax
import jax.numpy as jnp
from jax import lax
from jax.sharding import Mesh, PartitionSpec as P

NZ, NXL, NXH, NY, NC = 8, 2, 2, 4, 2
ALL = ("z", "xl", "xh", "y", "c")


def flat(z, xl, xh, y, c):
    return (((z % NZ * NXL + xl % NXL) * NXH + xh % NXH) * NY + y % NY) * NC + c % NC


def moved(array, where):
    pairs = []
    for z in range(NZ):
        for xl in range(NXL):
            for xh in range(NXH):
                for y in range(NY):
                    for c in range(NC):
                        target = where(z, xl, xh, y, c)
                        if target is not None:
                            pairs.append((flat(z, xl, xh, y, c), flat(*target)))
    return lax.ppermute(array, ALL, pairs)


def other_core(array):
    return moved(array, lambda z, xl, xh, y, c: (z, xl, xh, y, 1 - c))


def across(array):
    return moved(array, lambda z, xl, xh, y, c: (z, xl, 1 - xh, y, c))


def kind(xl, xh):
    return xl if xh == 0 else 1 - xl


def dot_nt(a, b):
    return lax.dot_general(a, b, (((1,), (1,)), ((), ())), preferred_element_type=jnp.float32)


def dot_nn(a, b):
    return lax.dot_general(a, b, (((1,), (0,)), ((), ())), preferred_element_type=jnp.float32)


def dot_tn(a, b):
    return lax.dot_general(a, b, (((0,), (0,)), ((), ())), preferred_element_type=jnp.float32)


def local(three_index, occ_energy, vir_energy):
    own = three_index[0]
    nvir, depth = own.shape
    share = nvir // NY
    c, xh, y = lax.axis_index("c"), lax.axis_index("xh"), lax.axis_index("y")

    high = lax.reduce_precision(occ_energy[0], 8, 7)
    rest = occ_energy[0] - high
    middle = lax.reduce_precision(rest, 8, 7)
    column = lax.broadcasted_iota(jnp.int32, (8, 4 * depth), 1)
    tail = jnp.where(column == 0, high, jnp.where(column == 1, middle, jnp.where(column == 2, rest - middle, 0.0)))
    there = across(own)
    beside = other_core(own)
    there_beside = other_core(there)

    def in_order(first, a, b):
        return jnp.where(first, jnp.concatenate([a, b], axis=1), jnp.concatenate([b, a], axis=1))

    mine = in_order(xh == 0, in_order(c == 0, own, beside), in_order(c == 0, there, there_beside))
    mine = jnp.concatenate([mine, tail.astype(jnp.bfloat16)], axis=0)

    step_one = moved(
        mine,
        lambda z, xl, xh, y, c: (z - 1, kind(xl, xh), xh, y, c) if c == 0 else (z + 1, xl, xh, y, c),
    )
    beyond = moved(mine, lambda z, xl, xh, y, c: (z, 1 - xl, 1, y, c) if (xh, c) == (0, 0) else None)
    swap_one = other_core(step_one)
    step_two = moved(step_one, lambda z, xl, xh, y, c: (z - 1 if c == 0 else z + 1, xl, xh, y, c))
    turned_one = moved(step_one, lambda z, xl, xh, y, c: (z, 1 - xl, 1, y, c) if (xh, c) == (0, 1) else None)

    def numer(a, b):
        a, b = a[:nvir], b[:nvir]
        return dot_nt(a * jnp.bfloat16(2), b) - dot_nt(b, a)

    def packed(*values):
        return jnp.stack([value.reshape(NY, share, nvir) for value in values], axis=1)

    def over_y(parts):
        return jnp.sum(lax.all_to_all(parts, "y", 0, 0, tiled=True), axis=0)

    def energy(block):
        terms = block[nvir, :3].astype(jnp.float32)
        return terms[0] + terms[1] + terms[2]

    vir_rows = lax.dynamic_slice_in_dim(vir_energy, y * share, share)
    virs = vir_rows[:, None] + vir_energy[None, :]

    def amps(value, a, b):
        return (value / (virs - energy(a) - energy(b))).astype(jnp.bfloat16)

    def to_all(*parts):
        parts = jnp.stack(parts)
        whole = lax.all_to_all(jnp.broadcast_to(parts, (NY, *parts.shape)), "y", 0, 0, tiled=True)
        return [whole[:, n].reshape(nvir, nvir) for n in range(parts.shape[0])]

    rows_one = jnp.where(c == 0, mine, step_one)
    cols_one = jnp.where(c == 0, step_one, swap_one)
    step_zero = jnp.where(xh == 0, mine, beyond)
    early = over_y(packed(numer(rows_one, cols_one), numer(mine, step_zero)))
    step_two, swap_one, early = lax.optimization_barrier((step_two, swap_one, early))
    swap_two = moved(step_two, lambda z, xl, xh, y, c: (z, xl, xh, y, 1) if c == 0 else None)
    rows_two = jnp.where(c == 0, swap_one, swap_two)
    late = over_y(packed(numer(rows_two, step_two)))

    turned_two = moved(turned_one, lambda z, xl, xh, y, c: (z + 1, xl, xh, y, c) if (xh, c) == (1, 1) else None)
    step_three = moved(
        step_two,
        lambda z, xl, xh, y, c: (z - 1, xl, xh, y, c) if c == 0 else (z + 1, kind(xl, xh), xh, y, c),
    )
    turned_four = moved(step_three, lambda z, xl, xh, y, c: (z + 1, xl, xh, y, 1) if c == 1 else None)

    amps_one = amps(early[0], rows_one, cols_one)
    amps_zero = amps(early[1], mine, step_zero)
    first = moved(
        amps_one,
        lambda z, xl, xh, y, c: (z + 1, kind(xl, xh), xh, y, 1) if c == 0 else (z - 1, xl, xh, y, 0),
    )
    second = moved(
        amps_one,
        lambda z, xl, xh, y, c: (z + 1, kind(xl, xh), xh, y, 1) if c == 1 else None,
    )
    second = jnp.where(c == 0, amps_one, second)
    late, first, second, step_three, amps_zero = lax.optimization_barrier((late, first, second, step_three, amps_zero))
    first, second = to_all(first, second)

    amps_two = amps(late[0], rows_two, step_two)
    third = moved(
        amps_two,
        lambda z, xl, xh, y, c: (z - 1, xl, xh, y, 0) if c == 0 else (z - 2, xl, xh, y, 1),
    )
    fourth = moved(amps_two, lambda z, xl, xh, y, c: (z + 2, kind(xl, xh), xh, y, 1) if c == 0 else None)
    fourth = jnp.where(c == 0, amps_zero, fourth)
    third, fourth, first, second = lax.optimization_barrier((third, fourth, first, second))
    third, fourth = to_all(third, fourth)

    width = NC * depth

    def product(h, k, parts, blocks, half):
        dot = dot_nn if k == 0 else dot_tn
        at = (1 - h if half == 0 else h) * width
        return sum(dot(part, block[:nvir, at : at + width]) for part, block in zip(parts, blocks))

    def both_halves(h, k, *blocks):
        return lambda parts: (product(h, k, parts, blocks, 0), product(h, k, parts, blocks, 1))

    def one_half(h, k, half, *blocks):
        def branch(parts, total):
            total = total + product(h, k, parts, blocks, half)
            cut = [total[:, n * depth : (n + 1) * depth] for n in range(NC)]
            return cut[1 - k], cut[k]

        return branch

    case = xh * NC + c
    halves = lax.switch(
        case,
        [
            both_halves(0, 0, step_two, step_one),
            both_halves(0, 1, step_one, step_two),
            both_halves(1, 0, step_two, step_one),
            both_halves(1, 1, turned_one, turned_two),
        ],
        (first, second),
    )

    def finished(half, begun):
        sent, kept = lax.switch(
            case,
            [
                one_half(0, 0, half, step_three, mine),
                one_half(0, 1, half, turned_four, step_three),
                one_half(1, 0, half, step_three, beyond),
                one_half(1, 1, half, turned_four, step_three),
            ],
            (third, fourth),
            begun,
        )
        return kept + other_core(sent)

    theirs, begun = lax.optimization_barrier((finished(0, halves[0]), halves[1]))
    got = across(theirs)
    return (finished(1, begun) + got)[None]


def solution(mesh):
    grid = Mesh(mesh.devices.reshape(NZ, NXL, NXH, NY, NC), ALL)
    return jax.shard_map(
        local,
        mesh=grid,
        in_specs=(P(("z", "xl"), None, ("xh", "y", "c")), P(("z", "xl")), P()),
        out_specs=P(("z", "xl"), None, ("xh", "y", "c")),
        check_vma=False,
    )
```

```python
import jax
import jax.numpy as jnp
from jax import lax
from jax.sharding import Mesh, PartitionSpec as P

NZ, NXL, NXH, NY, NC = 8, 2, 2, 4, 2
ALL = ("z", "xl", "xh", "y", "c")


def flat(z, xl, xh, y, c):
    return (((z % NZ * NXL + xl % NXL) * NXH + xh % NXH) * NY + y % NY) * NC + c % NC


def moved(array, where):
    pairs = []
    for z in range(NZ):
        for xl in range(NXL):
            for xh in range(NXH):
                for y in range(NY):
                    for c in range(NC):
                        target = where(z, xl, xh, y, c)
                        if target is not None:
                            pairs.append((flat(z, xl, xh, y, c), flat(*target)))
    return lax.ppermute(array, ALL, pairs)


def other_core(array):
    return moved(array, lambda z, xl, xh, y, c: (z, xl, xh, y, 1 - c))


def across(array):
    return moved(array, lambda z, xl, xh, y, c: (z, xl, 1 - xh, y, c))


def kind(xl, xh):
    return xl if xh == 0 else 1 - xl


def dot_nt(a, b):
    return lax.dot_general(a, b, (((1,), (1,)), ((), ())), preferred_element_type=jnp.float32)


def dot_nn(a, b):
    return lax.dot_general(a, b, (((1,), (0,)), ((), ())), preferred_element_type=jnp.float32)


def dot_tn(a, b):
    return lax.dot_general(a, b, (((0,), (0,)), ((), ())), preferred_element_type=jnp.float32)


def local(three_index, occ_energy, vir_energy):
    own = three_index[0]
    nvir, depth = own.shape
    share = nvir // NY
    c, xh, y = lax.axis_index("c"), lax.axis_index("xh"), lax.axis_index("y")

    high = lax.reduce_precision(occ_energy[0], 8, 7)
    rest = occ_energy[0] - high
    middle = lax.reduce_precision(rest, 8, 7)
    line = lax.broadcasted_iota(jnp.int32, (8, 4 * depth), 0)
    tail = jnp.where(line == 0, high, jnp.where(line == 1, middle, jnp.where(line == 2, rest - middle, 0.0)))
    there = across(own)
    beside = other_core(own)
    there_beside = other_core(there)

    def in_order(first, a, b):
        return jnp.where(first, jnp.concatenate([a, b], axis=1), jnp.concatenate([b, a], axis=1))

    mine = in_order(xh == 0, in_order(c == 0, own, beside), in_order(c == 0, there, there_beside))
    mine = jnp.concatenate([mine, tail.astype(jnp.bfloat16)], axis=0)

    step_one = moved(
        mine,
        lambda z, xl, xh, y, c: (z - 1, kind(xl, xh), xh, y, c) if c == 0 else (z + 1, xl, xh, y, c),
    )
    beyond = moved(mine, lambda z, xl, xh, y, c: (z, 1 - xl, 1, y, c) if (xh, c) == (0, 0) else None)
    swap_one = other_core(step_one)
    step_two = moved(step_one, lambda z, xl, xh, y, c: (z - 1 if c == 0 else z + 1, xl, xh, y, c))
    swap_two = moved(swap_one, lambda z, xl, xh, y, c: (z - 1, xl, xh, y, 1) if c == 1 else None)
    turned_one = moved(step_one, lambda z, xl, xh, y, c: (z, 1 - xl, 1, y, c) if (xh, c) == (0, 1) else None)

    def numer(a, b):
        a, b = a[:nvir], b[:nvir]
        return dot_nt(a * jnp.bfloat16(2), b) - dot_nt(b, a)

    def packed(*values):
        return jnp.stack([value.reshape(NY, share, nvir) for value in values], axis=1)

    def over_y(parts):
        return jnp.sum(lax.all_to_all(parts, "y", 0, 0, tiled=True), axis=0)

    def energy(block):
        terms = block[nvir:, :nvir].astype(jnp.float32)
        return terms[0:1] + terms[1:2] + terms[2:3]

    vir_rows = lax.dynamic_slice_in_dim(vir_energy, y * share, share)
    virs = vir_rows[:, None] + vir_energy[None, :]

    def amps(value, a, b):
        return (value / (virs - energy(a) - energy(b))).astype(jnp.bfloat16)

    def to_all(*parts):
        parts = jnp.stack(parts)
        whole = lax.all_to_all(jnp.broadcast_to(parts, (NY, *parts.shape)), "y", 0, 0, tiled=True)
        return [whole[:, n].reshape(nvir, nvir) for n in range(parts.shape[0])]

    rows_one = jnp.where(c == 0, mine, step_one)
    cols_one = jnp.where(c == 0, step_one, swap_one)
    step_zero = jnp.where(xh == 0, mine, beyond)
    early = over_y(packed(numer(rows_one, cols_one), numer(mine, step_zero)))
    step_two, swap_one, swap_two, early = lax.optimization_barrier((step_two, swap_one, swap_two, early))
    rows_two = jnp.where(c == 0, swap_one, swap_two)
    late = over_y(packed(numer(rows_two, step_two)))

    turned_two = moved(step_two, lambda z, xl, xh, y, c: (z, 1 - xl, 1, y, c) if (xh, c) == (0, 1) else None)
    step_three = moved(
        step_two,
        lambda z, xl, xh, y, c: (z - 1, xl, xh, y, c) if c == 0 else (z + 1, kind(xl, xh), xh, y, c),
    )
    turned_four = moved(step_three, lambda z, xl, xh, y, c: (z + 1, xl, xh, y, 1) if c == 1 else None)

    amps_one = amps(early[0], rows_one, cols_one)
    amps_zero = amps(early[1], mine, step_zero)
    first = moved(
        amps_one,
        lambda z, xl, xh, y, c: (z + 1, kind(xl, xh), xh, y, 1) if c == 0 else (z - 1, xl, xh, y, 0),
    )
    second = moved(
        amps_one,
        lambda z, xl, xh, y, c: (z + 1, kind(xl, xh), xh, y, 1) if c == 1 else None,
    )
    second = jnp.where(c == 0, amps_one, second)
    late, first, second, amps_zero = lax.optimization_barrier((late, first, second, amps_zero))
    first, second = to_all(first, second)

    amps_two = amps(late[0], rows_two, step_two)
    third = moved(
        amps_two,
        lambda z, xl, xh, y, c: (z - 1, xl, xh, y, 0) if c == 0 else (z - 2, xl, xh, y, 1),
    )
    fourth = moved(amps_two, lambda z, xl, xh, y, c: (z + 2, kind(xl, xh), xh, y, 1) if c == 0 else None)
    fourth = jnp.where(c == 0, amps_zero, fourth)
    third, fourth, first, second = lax.optimization_barrier((third, fourth, first, second))
    third, fourth = to_all(third, fourth)

    width = NC * depth

    def product(h, k, parts, blocks, half):
        dot = dot_nn if k == 0 else dot_tn
        at = (1 - h if half == 0 else h) * width
        return sum(dot(part, block[:nvir, at : at + width]) for part, block in zip(parts, blocks))

    def both_halves(h, k, *blocks):
        return lambda parts: (product(h, k, parts, blocks, 0), product(h, k, parts, blocks, 1))

    def one_half(h, k, half, *blocks):
        def branch(parts, total):
            total = total + product(h, k, parts, blocks, half)
            cut = [total[:, n * depth : (n + 1) * depth] for n in range(NC)]
            return cut[1 - k], cut[k]

        return branch

    case = xh * NC + c
    halves = lax.switch(
        case,
        [
            both_halves(0, 0, step_two, step_one),
            both_halves(0, 1, step_one, step_two),
            both_halves(1, 0, step_two, step_one),
            both_halves(1, 1, turned_one, turned_two),
        ],
        (first, second),
    )

    def finished(half, begun):
        sent, kept = lax.switch(
            case,
            [
                one_half(0, 0, half, step_three, mine),
                one_half(0, 1, half, turned_four, step_three),
                one_half(1, 0, half, step_three, beyond),
                one_half(1, 1, half, turned_four, step_three),
            ],
            (third, fourth),
            begun,
        )
        return kept + other_core(sent)

    theirs, begun = lax.optimization_barrier((finished(0, halves[0]), halves[1]))
    got = across(theirs)
    return (finished(1, begun) + got)[None]


def solution(mesh):
    grid = Mesh(mesh.devices.reshape(NZ, NXL, NXH, NY, NC), ALL)
    return jax.shard_map(
        local,
        mesh=grid,
        in_specs=(P(("z", "xl"), None, ("xh", "y", "c")), P(("z", "xl")), P()),
        out_specs=P(("z", "xl"), None, ("xh", "y", "c")),
        check_vma=False,
    )
```

```python
import jax
import jax.numpy as jnp
from jax import lax
from jax.sharding import Mesh, PartitionSpec as P

NZ, NXL, NXH, NY, NC = 8, 2, 2, 4, 2
ALL = ("z", "xl", "xh", "y", "c")


def flat(z, xl, xh, y, c):
    return (((z % NZ * NXL + xl % NXL) * NXH + xh % NXH) * NY + y % NY) * NC + c % NC


def moved(array, where):
    pairs = []
    for z in range(NZ):
        for xl in range(NXL):
            for xh in range(NXH):
                for y in range(NY):
                    for c in range(NC):
                        target = where(z, xl, xh, y, c)
                        if target is not None:
                            pairs.append((flat(z, xl, xh, y, c), flat(*target)))
    return lax.ppermute(array, ALL, pairs)


def other_core(array):
    return moved(array, lambda z, xl, xh, y, c: (z, xl, xh, y, 1 - c))


def across(array):
    return moved(array, lambda z, xl, xh, y, c: (z, xl, 1 - xh, y, c))


def kind(xl, xh):
    return xl if xh == 0 else 1 - xl


def dot_nt(a, b):
    return lax.dot_general(a, b, (((1,), (1,)), ((), ())), preferred_element_type=jnp.float32)


def dot_nn(a, b):
    return lax.dot_general(a, b, (((1,), (0,)), ((), ())), preferred_element_type=jnp.float32)


def dot_tn(a, b):
    return lax.dot_general(a, b, (((0,), (0,)), ((), ())), preferred_element_type=jnp.float32)


def local(three_index, occ_energy, vir_energy):
    own = three_index[0]
    nvir, depth = own.shape
    share = nvir // NY
    c, xh, y = lax.axis_index("c"), lax.axis_index("xh"), lax.axis_index("y")

    high = lax.reduce_precision(occ_energy[0], 8, 7)
    rest = occ_energy[0] - high
    middle = lax.reduce_precision(rest, 8, 7)
    line = lax.broadcasted_iota(jnp.int32, (8, 4 * depth), 0)
    tail = jnp.where(line == 0, high, jnp.where(line == 1, middle, jnp.where(line == 2, rest - middle, 0.0)))
    there = across(own)
    beside = other_core(own)
    there, tail = lax.optimization_barrier((there, tail.astype(jnp.bfloat16)))
    there_beside = other_core(there)

    def in_order(first, a, b):
        return jnp.where(first, jnp.concatenate([a, b], axis=1), jnp.concatenate([b, a], axis=1))

    mine = in_order(xh == 0, in_order(c == 0, own, beside), in_order(c == 0, there, there_beside))
    mine = jnp.concatenate([mine, tail], axis=0)

    step_one = moved(
        mine,
        lambda z, xl, xh, y, c: (z - 1, kind(xl, xh), xh, y, c) if c == 0 else (z + 1, xl, xh, y, c),
    )
    beyond = moved(mine, lambda z, xl, xh, y, c: (z, 1 - xl, 1, y, c) if (xh, c) == (0, 0) else None)
    swap_one = other_core(step_one)
    step_two = moved(step_one, lambda z, xl, xh, y, c: (z - 1 if c == 0 else z + 1, xl, xh, y, c))

    def numer(a, b):
        a, b = a[:nvir], b[:nvir]
        return dot_nt(a * jnp.bfloat16(2), b) - dot_nt(b, a)

    def packed(*values):
        return jnp.stack([value.reshape(NY, share, nvir) for value in values], axis=1)

    def over_y(parts):
        return jnp.sum(lax.all_to_all(parts, "y", 0, 0, tiled=True), axis=0)

    def energy(block):
        terms = block[nvir:, :nvir].astype(jnp.float32)
        return terms[0:1] + terms[1:2] + terms[2:3]

    vir_rows = lax.dynamic_slice_in_dim(vir_energy, y * share, share)
    virs = vir_rows[:, None] + vir_energy[None, :]

    def amps(value, a, b):
        return (value / (virs - energy(a) - energy(b))).astype(jnp.bfloat16)

    def to_all(*parts):
        parts = jnp.stack(parts)
        whole = lax.all_to_all(jnp.broadcast_to(parts, (NY, *parts.shape)), "y", 0, 0, tiled=True)
        return [whole[:, n].reshape(nvir, nvir) for n in range(parts.shape[0])]

    rows_one = jnp.where(c == 0, mine, step_one)
    cols_one = jnp.where(c == 0, step_one, swap_one)
    step_zero = jnp.where(xh == 0, mine, beyond)
    parts = packed(numer(rows_one, cols_one), numer(mine, step_zero))
    parts, swap_one, step_one_after = lax.optimization_barrier((parts, swap_one, step_one))
    swap_two = moved(swap_one, lambda z, xl, xh, y, c: (z - 1, xl, xh, y, 1) if c == 1 else None)
    turned_one = moved(step_one_after, lambda z, xl, xh, y, c: (z, 1 - xl, 1, y, c) if (xh, c) == (0, 1) else None)
    early = over_y(parts)
    step_two, swap_one, swap_two, early = lax.optimization_barrier((step_two, swap_one, swap_two, early))
    rows_two = jnp.where(c == 0, swap_one, swap_two)
    parts = packed(numer(rows_two, step_two))
    parts, early, step_two = lax.optimization_barrier((parts, early, step_two))
    late = over_y(parts)

    turned_two = moved(step_two, lambda z, xl, xh, y, c: (z, 1 - xl, 1, y, c) if (xh, c) == (0, 1) else None)
    step_three = moved(
        step_two,
        lambda z, xl, xh, y, c: (z - 1, xl, xh, y, c) if c == 0 else (z + 1, kind(xl, xh), xh, y, c),
    )
    turned_four = moved(step_three, lambda z, xl, xh, y, c: (z + 1, xl, xh, y, 1) if c == 1 else None)

    amps_one = amps(early[0], rows_one, cols_one)
    amps_zero = amps(early[1], mine, step_zero)
    first = moved(
        amps_one,
        lambda z, xl, xh, y, c: (z + 1, kind(xl, xh), xh, y, 1) if c == 0 else (z - 1, xl, xh, y, 0),
    )
    second = moved(
        amps_one,
        lambda z, xl, xh, y, c: (z + 1, kind(xl, xh), xh, y, 1) if c == 1 else None,
    )
    second = jnp.where(c == 0, amps_one, second)
    late, first, second, amps_zero, turned_one, turned_two = lax.optimization_barrier(
        (late, first, second, amps_zero, turned_one, turned_two)
    )
    amps_two = amps(late[0], rows_two, step_two)
    third = moved(
        amps_two,
        lambda z, xl, xh, y, c: (z - 1, xl, xh, y, 0) if c == 0 else (z - 2, xl, xh, y, 1),
    )
    fourth = moved(amps_two, lambda z, xl, xh, y, c: (z + 2, kind(xl, xh), xh, y, 1) if c == 0 else None)
    fourth = jnp.where(c == 0, amps_zero, fourth)
    pieces = to_all(first, second, third, fourth)

    width = NC * depth

    def product(h, k, parts, blocks, half):
        dot = dot_nn if k == 0 else dot_tn
        at = (1 - h if half == 0 else h) * width
        return sum(dot(part, block[:nvir, at : at + width]) for part, block in zip(parts, blocks))

    def one_half(h, k, half, *blocks):
        def branch(parts):
            total = product(h, k, parts, blocks, half)
            cut = [total[:, n * depth : (n + 1) * depth] for n in range(NC)]
            return cut[1 - k], cut[k]

        return branch

    def finished(half, parts):
        sent, kept = lax.switch(
            xh * NC + c,
            [
                one_half(0, 0, half, step_two, step_one, step_three, mine),
                one_half(0, 1, half, step_one, step_two, turned_four, step_three),
                one_half(1, 0, half, step_two, step_one, step_three, beyond),
                one_half(1, 1, half, turned_one, turned_two, turned_four, step_three),
            ],
            parts,
        )
        return kept + other_core(sent)

    theirs, pieces = lax.optimization_barrier((finished(0, pieces), pieces))
    got = across(theirs)
    return (finished(1, pieces) + got)[None]


def solution(mesh):
    grid = Mesh(mesh.devices.reshape(NZ, NXL, NXH, NY, NC), ALL)
    return jax.shard_map(
        local,
        mesh=grid,
        in_specs=(P(("z", "xl"), None, ("xh", "y", "c")), P(("z", "xl")), P()),
        out_specs=P(("z", "xl"), None, ("xh", "y", "c")),
        check_vma=False,
    )
```

```python
import jax
import jax.numpy as jnp
from jax import lax
from jax.sharding import Mesh, PartitionSpec as P

NZ, NXL, NXH, NY, NC = 8, 2, 2, 4, 2
ALL = ("z", "xl", "xh", "y", "c")


def flat(z, xl, xh, y, c):
    return (((z % NZ * NXL + xl % NXL) * NXH + xh % NXH) * NY + y % NY) * NC + c % NC


def moved(array, where):
    pairs = []
    for z in range(NZ):
        for xl in range(NXL):
            for xh in range(NXH):
                for y in range(NY):
                    for c in range(NC):
                        target = where(z, xl, xh, y, c)
                        if target is not None:
                            pairs.append((flat(z, xl, xh, y, c), flat(*target)))
    return lax.ppermute(array, ALL, pairs)


def other_core(array):
    return moved(array, lambda z, xl, xh, y, c: (z, xl, xh, y, 1 - c))


def across(array):
    return moved(array, lambda z, xl, xh, y, c: (z, xl, 1 - xh, y, c))


def kind(xl, xh):
    return xl if xh == 0 else 1 - xl


def dot_nt(a, b):
    return lax.dot_general(a, b, (((1,), (1,)), ((), ())), preferred_element_type=jnp.float32)


def dot_nn(a, b):
    return lax.dot_general(a, b, (((1,), (0,)), ((), ())), preferred_element_type=jnp.float32)


def dot_tn(a, b):
    return lax.dot_general(a, b, (((0,), (0,)), ((), ())), preferred_element_type=jnp.float32)


def local(three_index, occ_energy, vir_energy):
    own = three_index[0]
    nvir, depth = own.shape
    share = nvir // NY
    c, xh, y = lax.axis_index("c"), lax.axis_index("xh"), lax.axis_index("y")

    high = lax.reduce_precision(occ_energy[0], 8, 7)
    rest = occ_energy[0] - high
    middle = lax.reduce_precision(rest, 8, 7)
    line = lax.broadcasted_iota(jnp.int32, (8, 4 * depth), 0)
    tail = jnp.where(line == 0, high, jnp.where(line == 1, middle, jnp.where(line == 2, rest - middle, 0.0)))
    there = across(own)
    beside = other_core(own)
    there, tail = lax.optimization_barrier((there, tail.astype(jnp.bfloat16)))
    there_beside = other_core(there)

    def in_order(first, a, b):
        return jnp.where(first, jnp.concatenate([a, b], axis=1), jnp.concatenate([b, a], axis=1))

    mine = in_order(xh == 0, in_order(c == 0, own, beside), in_order(c == 0, there, there_beside))
    mine = jnp.concatenate([mine, tail], axis=0)

    step_one = moved(
        mine,
        lambda z, xl, xh, y, c: (z - 1, kind(xl, xh), xh, y, c) if c == 0 else (z + 1, xl, xh, y, c),
    )
    beyond = moved(mine, lambda z, xl, xh, y, c: (z, 1 - xl, 1, y, c) if (xh, c) == (0, 0) else None)
    swap_one = other_core(step_one)
    step_two = moved(step_one, lambda z, xl, xh, y, c: (z - 1 if c == 0 else z + 1, xl, xh, y, c))

    def numer(a, b):
        a, b = a[:nvir], b[:nvir]
        return dot_nt(a * jnp.bfloat16(2), b) - dot_nt(b, a)

    def packed(*values):
        return jnp.stack([value.reshape(NY, share, nvir) for value in values], axis=1)

    def over_y(parts):
        return jnp.sum(lax.all_to_all(parts, "y", 0, 0, tiled=True), axis=0)

    def energy(block):
        terms = block[nvir:, :nvir].astype(jnp.float32)
        return terms[0:1] + terms[1:2] + terms[2:3]

    vir_rows = lax.dynamic_slice_in_dim(vir_energy, y * share, share)
    virs = vir_rows[:, None] + vir_energy[None, :]

    def amps(value, a, b):
        return (value / (virs - energy(a) - energy(b))).astype(jnp.bfloat16)

    def to_all(*parts):
        parts = jnp.stack(parts)
        whole = lax.all_to_all(jnp.broadcast_to(parts, (NY, *parts.shape)), "y", 0, 0, tiled=True)
        return [whole[:, n].reshape(nvir, nvir) for n in range(parts.shape[0])]

    rows_one = jnp.where(c == 0, mine, step_one)
    cols_one = jnp.where(c == 0, step_one, swap_one)
    step_zero = jnp.where(xh == 0, mine, beyond)
    parts = packed(numer(rows_one, cols_one), numer(mine, step_zero))
    parts, swap_one, step_one_after = lax.optimization_barrier((parts, swap_one, step_one))
    swap_two = moved(swap_one, lambda z, xl, xh, y, c: (z - 1, xl, xh, y, 1) if c == 1 else None)
    turned_one = moved(step_one_after, lambda z, xl, xh, y, c: (z, 1 - xl, 1, y, c) if (xh, c) == (0, 1) else None)
    early = over_y(parts)
    step_two, swap_one, swap_two, early = lax.optimization_barrier((step_two, swap_one, swap_two, early))
    rows_two = jnp.where(c == 0, swap_one, swap_two)
    late = over_y(packed(numer(rows_two, step_two)))

    amps_one = amps(early[0], rows_one, cols_one)
    amps_zero = amps(early[1], mine, step_zero)
    first = moved(
        amps_one,
        lambda z, xl, xh, y, c: (z + 1, kind(xl, xh), xh, y, 1) if c == 0 else (z - 1, xl, xh, y, 0),
    )
    second = moved(
        amps_one,
        lambda z, xl, xh, y, c: (z + 1, kind(xl, xh), xh, y, 1) if c == 1 else None,
    )
    second = jnp.where(c == 0, amps_one, second)
    late, first, second, amps_zero, step_two, turned_one = lax.optimization_barrier(
        (late, first, second, amps_zero, step_two, turned_one)
    )

    turned_two = moved(step_two, lambda z, xl, xh, y, c: (z, 1 - xl, 1, y, c) if (xh, c) == (0, 1) else None)
    step_three = moved(
        step_two,
        lambda z, xl, xh, y, c: (z - 1, xl, xh, y, c) if c == 0 else (z + 1, kind(xl, xh), xh, y, c),
    )
    turned_four = moved(step_three, lambda z, xl, xh, y, c: (z + 1, xl, xh, y, 1) if c == 1 else None)
    first, second = to_all(first, second)

    amps_two = amps(late[0], rows_two, step_two)
    third = moved(
        amps_two,
        lambda z, xl, xh, y, c: (z - 1, xl, xh, y, 0) if c == 0 else (z - 2, xl, xh, y, 1),
    )
    fourth = moved(amps_two, lambda z, xl, xh, y, c: (z + 2, kind(xl, xh), xh, y, 1) if c == 0 else None)
    fourth = jnp.where(c == 0, amps_zero, fourth)
    third, fourth, first, second, turned_two = lax.optimization_barrier((third, fourth, first, second, turned_two))
    third, fourth = to_all(third, fourth)

    width = NC * depth

    def product(h, k, parts, blocks, half):
        dot = dot_nn if k == 0 else dot_tn
        at = (1 - h if half == 0 else h) * width
        return sum(dot(part, block[:nvir, at : at + width]) for part, block in zip(parts, blocks))

    def both_halves(h, k, *blocks):
        return lambda parts: (product(h, k, parts, blocks, 0), product(h, k, parts, blocks, 1))

    def one_half(h, k, half, *blocks):
        def branch(parts, total):
            total = total + product(h, k, parts, blocks, half)
            cut = [total[:, n * depth : (n + 1) * depth] for n in range(NC)]
            return cut[1 - k], cut[k]

        return branch

    case = xh * NC + c
    halves = lax.switch(
        case,
        [
            both_halves(0, 0, step_two, step_one),
            both_halves(0, 1, step_one, step_two),
            both_halves(1, 0, step_two, step_one),
            both_halves(1, 1, turned_one, turned_two),
        ],
        (first, second),
    )

    def finished(half, begun):
        sent, kept = lax.switch(
            case,
            [
                one_half(0, 0, half, step_three, mine),
                one_half(0, 1, half, turned_four, step_three),
                one_half(1, 0, half, step_three, beyond),
                one_half(1, 1, half, turned_four, step_three),
            ],
            (third, fourth),
            begun,
        )
        return kept + other_core(sent)

    theirs, begun = lax.optimization_barrier((finished(0, halves[0]), halves[1]))
    got = across(theirs)
    return (finished(1, begun) + got)[None]


def solution(mesh):
    grid = Mesh(mesh.devices.reshape(NZ, NXL, NXH, NY, NC), ALL)
    return jax.shard_map(
        local,
        mesh=grid,
        in_specs=(P(("z", "xl"), None, ("xh", "y", "c")), P(("z", "xl")), P()),
        out_specs=P(("z", "xl"), None, ("xh", "y", "c")),
        check_vma=False,
    )
```

```python
import jax
import jax.numpy as jnp
from jax import lax
from jax.experimental import pallas as pl
from jax.experimental.pallas import tpu as pltpu
from jax.sharding import Mesh, PartitionSpec as P

NZ, NXL, NXH, NY, NC = 8, 2, 2, 4, 2
ALL = ("z", "xl", "xh", "y", "c")


def flat(z, xl, xh, y, c):
    return (((z % NZ * NXL + xl % NXL) * NXH + xh % NXH) * NY + y % NY) * NC + c % NC


def moved(array, where):
    pairs = []
    for z in range(NZ):
        for xl in range(NXL):
            for xh in range(NXH):
                for y in range(NY):
                    for c in range(NC):
                        target = where(z, xl, xh, y, c)
                        if target is not None:
                            pairs.append((flat(z, xl, xh, y, c), flat(*target)))
    return lax.ppermute(array, ALL, pairs)


def other_core(array):
    return moved(array, lambda z, xl, xh, y, c: (z, xl, xh, y, 1 - c))


def across(array):
    return moved(array, lambda z, xl, xh, y, c: (z, xl, 1 - xh, y, c))


def kind(xl, xh):
    return xl if xh == 0 else 1 - xl


def dot_nt(a, b):
    return lax.dot_general(a, b, (((1,), (1,)), ((), ())), preferred_element_type=jnp.float32)


def dot_nn(a, b):
    return lax.dot_general(a, b, (((1,), (0,)), ((), ())), preferred_element_type=jnp.float32)


def dot_tn(a, b):
    return lax.dot_general(a, b, (((0,), (0,)), ((), ())), preferred_element_type=jnp.float32)


def numer_into(a_ref, b_ref, out_ref, slot):
    nvir = out_ref.shape[3]
    a, b = a_ref[:nvir, :], b_ref[:nvir, :]
    value = 2.0 * dot_nt(a, b) - dot_nt(b, a)
    out_ref[:, slot] = value.reshape(out_ref.shape[0], out_ref.shape[2], nvir)


def early_kernel(where_ref, mine_ref, one_ref, swap_ref, beyond_ref, out_ref):
    @pl.when(where_ref[0] == 0)
    def _():
        numer_into(mine_ref, one_ref, out_ref, 0)

    @pl.when(where_ref[0] != 0)
    def _():
        numer_into(one_ref, swap_ref, out_ref, 0)

    @pl.when(where_ref[1] == 0)
    def _():
        numer_into(mine_ref, mine_ref, out_ref, 1)

    @pl.when(where_ref[1] != 0)
    def _():
        numer_into(mine_ref, beyond_ref, out_ref, 1)


def late_kernel(where_ref, swap_one_ref, swap_two_ref, two_ref, out_ref):
    @pl.when(where_ref[0] == 0)
    def _():
        numer_into(swap_one_ref, two_ref, out_ref, 0)

    @pl.when(where_ref[0] != 0)
    def _():
        numer_into(swap_two_ref, two_ref, out_ref, 0)


def numerators(kernel, count, where, nvir, *blocks):
    share = nvir // NY
    width = blocks[0].shape[1]
    return pl.pallas_call(
        kernel,
        out_shape=jax.ShapeDtypeStruct((NY, count, share, nvir), jnp.float32),
        in_specs=[pl.BlockSpec(memory_space=pltpu.SMEM)] + [pl.BlockSpec(memory_space=pltpu.VMEM)] * len(blocks),
        out_specs=pl.BlockSpec(memory_space=pltpu.VMEM),
        cost_estimate=pl.CostEstimate(
            flops=4 * count * nvir * nvir * width,
            bytes_accessed=2 * len(blocks) * nvir * width + 4 * count * nvir * nvir,
            transcendentals=0,
        ),
        compiler_params=pltpu.CompilerParams(vmem_limit_bytes=24 * 2**20),
    )(where, *blocks)


def local(three_index, occ_energy, vir_energy):
    own = three_index[0]
    nvir, depth = own.shape
    share = nvir // NY
    c, xh, y = lax.axis_index("c"), lax.axis_index("xh"), lax.axis_index("y")

    high = lax.reduce_precision(occ_energy[0], 8, 7)
    rest = occ_energy[0] - high
    middle = lax.reduce_precision(rest, 8, 7)
    line = lax.broadcasted_iota(jnp.int32, (8, 4 * depth), 0)
    tail = jnp.where(line == 0, high, jnp.where(line == 1, middle, jnp.where(line == 2, rest - middle, 0.0)))
    there = across(own)
    beside = other_core(own)
    there, tail = lax.optimization_barrier((there, tail.astype(jnp.bfloat16)))
    there_beside = other_core(there)

    def in_order(first, a, b):
        return jnp.where(first, jnp.concatenate([a, b], axis=1), jnp.concatenate([b, a], axis=1))

    mine = in_order(xh == 0, in_order(c == 0, own, beside), in_order(c == 0, there, there_beside))
    mine = jnp.concatenate([mine, tail], axis=0)

    step_one = moved(
        mine,
        lambda z, xl, xh, y, c: (z - 1, kind(xl, xh), xh, y, c) if c == 0 else (z + 1, xl, xh, y, c),
    )
    beyond = moved(mine, lambda z, xl, xh, y, c: (z, 1 - xl, 1, y, c) if (xh, c) == (0, 0) else None)
    swap_one = other_core(step_one)
    step_two = moved(step_one, lambda z, xl, xh, y, c: (z - 1 if c == 0 else z + 1, xl, xh, y, c))

    def over_y(parts):
        return jnp.sum(lax.all_to_all(parts, "y", 0, 0, tiled=True), axis=0)

    def energy(block):
        terms = block[nvir:, :nvir].astype(jnp.float32)
        return terms[0:1] + terms[1:2] + terms[2:3]

    vir_rows = lax.dynamic_slice_in_dim(vir_energy, y * share, share)
    virs = vir_rows[:, None] + vir_energy[None, :]

    def amps(value, a, b):
        return (value / (virs - a - b)).astype(jnp.bfloat16)

    def to_all(*parts):
        parts = jnp.stack(parts)
        whole = lax.all_to_all(jnp.broadcast_to(parts, (NY, *parts.shape)), "y", 0, 0, tiled=True)
        return [whole[:, n].reshape(nvir, nvir) for n in range(parts.shape[0])]

    where = jnp.stack([c, xh])
    parts = numerators(early_kernel, 2, where, nvir, mine, step_one, swap_one, beyond)
    parts, swap_one, step_one_after = lax.optimization_barrier((parts, swap_one, step_one))
    swap_two = moved(swap_one, lambda z, xl, xh, y, c: (z - 1, xl, xh, y, 1) if c == 1 else None)
    turned_one = moved(step_one_after, lambda z, xl, xh, y, c: (z, 1 - xl, 1, y, c) if (xh, c) == (0, 1) else None)
    early = over_y(parts)
    step_two, swap_one, swap_two, early = lax.optimization_barrier((step_two, swap_one, swap_two, early))
    late = over_y(numerators(late_kernel, 1, where, nvir, swap_one, swap_two, step_two))

    mine_energy, one_energy, swap_energy = energy(mine), energy(step_one), energy(swap_one)
    amps_one = amps(
        early[0], jnp.where(c == 0, mine_energy, one_energy), jnp.where(c == 0, one_energy, swap_energy)
    )
    amps_zero = amps(early[1], mine_energy, jnp.where(xh == 0, mine_energy, energy(beyond)))
    first = moved(
        amps_one,
        lambda z, xl, xh, y, c: (z + 1, kind(xl, xh), xh, y, 1) if c == 0 else (z - 1, xl, xh, y, 0),
    )
    second = moved(
        amps_one,
        lambda z, xl, xh, y, c: (z + 1, kind(xl, xh), xh, y, 1) if c == 1 else None,
    )
    second = jnp.where(c == 0, amps_one, second)
    late, first, second, amps_zero, step_two, turned_one = lax.optimization_barrier(
        (late, first, second, amps_zero, step_two, turned_one)
    )

    turned_two = moved(step_two, lambda z, xl, xh, y, c: (z, 1 - xl, 1, y, c) if (xh, c) == (0, 1) else None)
    step_three = moved(
        step_two,
        lambda z, xl, xh, y, c: (z - 1, xl, xh, y, c) if c == 0 else (z + 1, kind(xl, xh), xh, y, c),
    )
    turned_four = moved(step_three, lambda z, xl, xh, y, c: (z + 1, xl, xh, y, 1) if c == 1 else None)
    first, second = to_all(first, second)

    amps_two = amps(late[0], jnp.where(c == 0, swap_energy, energy(swap_two)), energy(step_two))
    third = moved(
        amps_two,
        lambda z, xl, xh, y, c: (z - 1, xl, xh, y, 0) if c == 0 else (z - 2, xl, xh, y, 1),
    )
    fourth = moved(amps_two, lambda z, xl, xh, y, c: (z + 2, kind(xl, xh), xh, y, 1) if c == 0 else None)
    fourth = jnp.where(c == 0, amps_zero, fourth)
    third, fourth, first, second, turned_two = lax.optimization_barrier((third, fourth, first, second, turned_two))
    third, fourth = to_all(third, fourth)

    def product(dot, *blocks):
        return lambda parts: sum(dot(part, block[:nvir]) for part, block in zip(parts, blocks))

    case = xh * NC + c
    begun = lax.switch(
        case,
        [
            product(dot_nn, step_two, step_one),
            product(dot_tn, step_one, step_two),
            product(dot_nn, step_two, step_one),
            product(dot_tn, turned_one, turned_two),
        ],
        (first, second),
    )

    def ending(h, k, dot, *blocks):
        def branch(parts, total):
            total = total + product(dot, *blocks)(parts)
            cut = [total[:, n * depth : (n + 1) * depth] for n in range(NXH * NC)]
            sent = jnp.concatenate([cut[NC * (1 - h) + 1 - k], cut[NC * h + 1 - k]], axis=1)
            return sent, cut[NC * (1 - h) + k], cut[NC * h + k]

        return branch

    sent, theirs, ours = lax.switch(
        case,
        [
            ending(0, 0, dot_nn, step_three, mine),
            ending(0, 1, dot_tn, turned_four, step_three),
            ending(1, 0, dot_nn, step_three, beyond),
            ending(1, 1, dot_tn, turned_four, step_three),
        ],
        (third, fourth),
        begun,
    )
    got = other_core(sent)
    return (ours + got[:, depth:] + across(theirs + got[:, :depth]))[None]


def solution(mesh):
    grid = Mesh(mesh.devices.reshape(NZ, NXL, NXH, NY, NC), ALL)
    return jax.shard_map(
        local,
        mesh=grid,
        in_specs=(P(("z", "xl"), None, ("xh", "y", "c")), P(("z", "xl")), P()),
        out_specs=P(("z", "xl"), None, ("xh", "y", "c")),
        check_vma=False,
    )
```

```python
import jax
import jax.numpy as jnp
from jax import lax
from jax.experimental import pallas as pl
from jax.experimental.pallas import tpu as pltpu
from jax.sharding import Mesh, PartitionSpec as P

NZ, NXL, NXH, NY, NC = 8, 2, 2, 4, 2
ALL = ("z", "xl", "xh", "y", "c")


def flat(z, xl, xh, y, c):
    return (((z % NZ * NXL + xl % NXL) * NXH + xh % NXH) * NY + y % NY) * NC + c % NC


def moved(array, where):
    pairs = []
    for z in range(NZ):
        for xl in range(NXL):
            for xh in range(NXH):
                for y in range(NY):
                    for c in range(NC):
                        target = where(z, xl, xh, y, c)
                        if target is not None:
                            pairs.append((flat(z, xl, xh, y, c), flat(*target)))
    return lax.ppermute(array, ALL, pairs)


def other_core(array):
    return moved(array, lambda z, xl, xh, y, c: (z, xl, xh, y, 1 - c))


def across(array):
    return moved(array, lambda z, xl, xh, y, c: (z, xl, 1 - xh, y, c))


def kind(xl, xh):
    return xl if xh == 0 else 1 - xl


def dot_nt(a, b):
    return lax.dot_general(a, b, (((1,), (1,)), ((), ())), preferred_element_type=jnp.float32)


def dot_nn(a, b):
    return lax.dot_general(a, b, (((1,), (0,)), ((), ())), preferred_element_type=jnp.float32)


def dot_tn(a, b):
    return lax.dot_general(a, b, (((0,), (0,)), ((), ())), preferred_element_type=jnp.float32)


def numer_into(a_ref, b_ref, out_ref, slot):
    nvir = out_ref.shape[3]
    a, b = a_ref[:nvir, :], b_ref[:nvir, :]
    value = 2.0 * dot_nt(a, b) - dot_nt(b, a)
    out_ref[:, slot] = value.reshape(out_ref.shape[0], out_ref.shape[2], nvir)


def early_kernel(where_ref, mine_ref, one_ref, swap_ref, beyond_ref, out_ref):
    @pl.when(where_ref[0] == 0)
    def _():
        numer_into(mine_ref, one_ref, out_ref, 0)

    @pl.when(where_ref[0] != 0)
    def _():
        numer_into(one_ref, swap_ref, out_ref, 0)

    @pl.when(where_ref[1] == 0)
    def _():
        numer_into(mine_ref, mine_ref, out_ref, 1)

    @pl.when(where_ref[1] != 0)
    def _():
        numer_into(mine_ref, beyond_ref, out_ref, 1)


def late_kernel(where_ref, swap_one_ref, swap_two_ref, two_ref, out_ref):
    @pl.when(where_ref[0] == 0)
    def _():
        numer_into(swap_one_ref, two_ref, out_ref, 0)

    @pl.when(where_ref[0] != 0)
    def _():
        numer_into(swap_two_ref, two_ref, out_ref, 0)


def numerators(kernel, count, where, nvir, *blocks):
    share = nvir // NY
    width = blocks[0].shape[1]
    return pl.pallas_call(
        kernel,
        out_shape=jax.ShapeDtypeStruct((NY, count, share, nvir), jnp.float32),
        in_specs=[pl.BlockSpec(memory_space=pltpu.SMEM)] + [pl.BlockSpec(memory_space=pltpu.VMEM)] * len(blocks),
        out_specs=pl.BlockSpec(memory_space=pltpu.VMEM),
        cost_estimate=pl.CostEstimate(
            flops=4 * count * nvir * nvir * width,
            bytes_accessed=2 * len(blocks) * nvir * width + 4 * count * nvir * nvir,
            transcendentals=0,
        ),
        compiler_params=pltpu.CompilerParams(vmem_limit_bytes=24 * 2**20),
    )(where, *blocks)


def local(three_index, occ_energy, vir_energy):
    own = three_index[0]
    nvir, depth = own.shape
    share = nvir // NY
    c, xh, y = lax.axis_index("c"), lax.axis_index("xh"), lax.axis_index("y")

    high = lax.reduce_precision(occ_energy[0], 8, 7)
    rest = occ_energy[0] - high
    middle = lax.reduce_precision(rest, 8, 7)
    line = lax.broadcasted_iota(jnp.int32, (8, 4 * depth), 0)
    tail = jnp.where(line == 0, high, jnp.where(line == 1, middle, jnp.where(line == 2, rest - middle, 0.0)))
    there = across(own)
    beside = other_core(own)
    there, tail = lax.optimization_barrier((there, tail.astype(jnp.bfloat16)))
    there_beside = other_core(there)

    def in_order(first, a, b):
        return jnp.where(first, jnp.concatenate([a, b], axis=1), jnp.concatenate([b, a], axis=1))

    mine = in_order(xh == 0, in_order(c == 0, own, beside), in_order(c == 0, there, there_beside))
    mine = jnp.concatenate([mine, tail], axis=0)

    step_one = moved(
        mine,
        lambda z, xl, xh, y, c: (z - 1, kind(xl, xh), xh, y, c) if c == 0 else (z + 1, xl, xh, y, c),
    )
    beyond = moved(mine, lambda z, xl, xh, y, c: (z, 1 - xl, 1, y, c) if (xh, c) == (0, 0) else None)
    swap_one = other_core(step_one)
    step_two = moved(step_one, lambda z, xl, xh, y, c: (z - 1 if c == 0 else z + 1, xl, xh, y, c))

    def over_y(parts):
        return jnp.sum(lax.all_to_all(parts, "y", 0, 0, tiled=True), axis=0)

    def energy(block):
        terms = block[nvir:, :nvir].astype(jnp.float32)
        return terms[0:1] + terms[1:2] + terms[2:3]

    vir_rows = lax.dynamic_slice_in_dim(vir_energy, y * share, share)
    virs = vir_rows[:, None] + vir_energy[None, :]

    def amps(value, a, b):
        return (value / (virs - a - b)).astype(jnp.bfloat16)

    def to_all(*parts):
        parts = jnp.stack(parts)
        whole = lax.all_to_all(jnp.broadcast_to(parts, (NY, *parts.shape)), "y", 0, 0, tiled=True)
        return [whole[:, n].reshape(nvir, nvir) for n in range(parts.shape[0])]

    where = jnp.stack([c, xh])
    parts = numerators(early_kernel, 2, where, nvir, mine, step_one, swap_one, beyond)
    parts, swap_one, step_one_after = lax.optimization_barrier((parts, swap_one, step_one))
    swap_two = moved(swap_one, lambda z, xl, xh, y, c: (z - 1, xl, xh, y, 1) if c == 1 else None)
    turned_one = moved(step_one_after, lambda z, xl, xh, y, c: (z, 1 - xl, 1, y, c) if (xh, c) == (0, 1) else None)
    early = over_y(parts)
    turned_two = moved(step_two, lambda z, xl, xh, y, c: (z, 1 - xl, 1, y, c) if (xh, c) == (0, 1) else None)
    step_three = moved(
        step_two,
        lambda z, xl, xh, y, c: (z - 1, xl, xh, y, c) if c == 0 else (z + 1, kind(xl, xh), xh, y, c),
    )
    turned_four = moved(step_three, lambda z, xl, xh, y, c: (z + 1, xl, xh, y, 1) if c == 1 else None)

    step_two, swap_one, swap_two, early = lax.optimization_barrier((step_two, swap_one, swap_two, early))
    late = over_y(numerators(late_kernel, 1, where, nvir, swap_one, swap_two, step_two))

    mine_energy, one_energy, swap_energy = energy(mine), energy(step_one), energy(swap_one)
    amps_one = amps(
        early[0], jnp.where(c == 0, mine_energy, one_energy), jnp.where(c == 0, one_energy, swap_energy)
    )
    amps_zero = amps(early[1], mine_energy, jnp.where(xh == 0, mine_energy, energy(beyond)))
    first = moved(
        amps_one,
        lambda z, xl, xh, y, c: (z + 1, kind(xl, xh), xh, y, 1) if c == 0 else (z - 1, xl, xh, y, 0),
    )
    second = moved(
        amps_one,
        lambda z, xl, xh, y, c: (z + 1, kind(xl, xh), xh, y, 1) if c == 1 else None,
    )
    second = jnp.where(c == 0, amps_one, second)
    late, first, second, amps_zero, turned_one, turned_two, step_three = lax.optimization_barrier(
        (late, first, second, amps_zero, turned_one, turned_two, step_three)
    )

    first, second = to_all(first, second)

    amps_two = amps(late[0], jnp.where(c == 0, swap_energy, energy(swap_two)), energy(step_two))
    third = moved(
        amps_two,
        lambda z, xl, xh, y, c: (z - 1, xl, xh, y, 0) if c == 0 else (z - 2, xl, xh, y, 1),
    )
    fourth = moved(amps_two, lambda z, xl, xh, y, c: (z + 2, kind(xl, xh), xh, y, 1) if c == 0 else None)
    fourth = jnp.where(c == 0, amps_zero, fourth)
    third, fourth, first, second, turned_two = lax.optimization_barrier((third, fourth, first, second, turned_two))
    third, fourth = to_all(third, fourth)

    def product(dot, *blocks):
        return lambda parts: sum(dot(part, block[:nvir]) for part, block in zip(parts, blocks))

    case = xh * NC + c
    begun = lax.switch(
        case,
        [
            product(dot_nn, step_two, step_one),
            product(dot_tn, step_one, step_two),
            product(dot_nn, step_two, step_one),
            product(dot_tn, turned_one, turned_two),
        ],
        (first, second),
    )

    def ending(h, k, dot, *blocks):
        def branch(parts, total):
            total = total + product(dot, *blocks)(parts)
            cut = [total[:, n * depth : (n + 1) * depth] for n in range(NXH * NC)]
            sent = jnp.concatenate([cut[NC * (1 - h) + 1 - k], cut[NC * h + 1 - k]], axis=1)
            return sent, cut[NC * (1 - h) + k], cut[NC * h + k]

        return branch

    sent, theirs, ours = lax.switch(
        case,
        [
            ending(0, 0, dot_nn, step_three, mine),
            ending(0, 1, dot_tn, turned_four, step_three),
            ending(1, 0, dot_nn, step_three, beyond),
            ending(1, 1, dot_tn, turned_four, step_three),
        ],
        (third, fourth),
        begun,
    )
    got = other_core(sent)
    return (ours + got[:, depth:] + across(theirs + got[:, :depth]))[None]


def solution(mesh):
    grid = Mesh(mesh.devices.reshape(NZ, NXL, NXH, NY, NC), ALL)
    return jax.shard_map(
        local,
        mesh=grid,
        in_specs=(P(("z", "xl"), None, ("xh", "y", "c")), P(("z", "xl")), P()),
        out_specs=P(("z", "xl"), None, ("xh", "y", "c")),
        check_vma=False,
    )
```

```python
import jax
import jax.numpy as jnp
from jax import lax
from jax.experimental import pallas as pl
from jax.experimental.pallas import tpu as pltpu
from jax.sharding import Mesh, PartitionSpec as P

NZ, NXL, NXH, NY, NC = 8, 2, 2, 4, 2
ALL = ("z", "xl", "xh", "y", "c")


def flat(z, xl, xh, y, c):
    return (((z % NZ * NXL + xl % NXL) * NXH + xh % NXH) * NY + y % NY) * NC + c % NC


def moved(array, where):
    pairs = []
    for z in range(NZ):
        for xl in range(NXL):
            for xh in range(NXH):
                for y in range(NY):
                    for c in range(NC):
                        target = where(z, xl, xh, y, c)
                        if target is not None:
                            pairs.append((flat(z, xl, xh, y, c), flat(*target)))
    return lax.ppermute(array, ALL, pairs)


def other_core(array):
    return moved(array, lambda z, xl, xh, y, c: (z, xl, xh, y, 1 - c))


def across(array):
    return moved(array, lambda z, xl, xh, y, c: (z, xl, 1 - xh, y, c))


def kind(xl, xh):
    return xl if xh == 0 else 1 - xl


def dot_nt(a, b):
    return lax.dot_general(a, b, (((1,), (1,)), ((), ())), preferred_element_type=jnp.float32)


def dot_nn(a, b):
    return lax.dot_general(a, b, (((1,), (0,)), ((), ())), preferred_element_type=jnp.float32)


def dot_tn(a, b):
    return lax.dot_general(a, b, (((0,), (0,)), ((), ())), preferred_element_type=jnp.float32)


def numer_into(a_ref, b_ref, out_ref, slot):
    nvir = out_ref.shape[3]
    a, b = a_ref[:nvir, :], b_ref[:nvir, :]
    value = 2.0 * dot_nt(a, b) - dot_nt(b, a)
    out_ref[:, slot] = value.reshape(out_ref.shape[0], out_ref.shape[2], nvir)


def early_kernel(where_ref, mine_ref, one_ref, swap_ref, beyond_ref, out_ref):
    @pl.when(where_ref[0] == 0)
    def _():
        numer_into(mine_ref, one_ref, out_ref, 0)

    @pl.when(where_ref[0] != 0)
    def _():
        numer_into(one_ref, swap_ref, out_ref, 0)

    @pl.when(where_ref[1] == 0)
    def _():
        numer_into(mine_ref, mine_ref, out_ref, 1)

    @pl.when(where_ref[1] != 0)
    def _():
        numer_into(mine_ref, beyond_ref, out_ref, 1)


def late_kernel(where_ref, swap_one_ref, swap_two_ref, two_ref, out_ref):
    @pl.when(where_ref[0] == 0)
    def _():
        numer_into(swap_one_ref, two_ref, out_ref, 0)

    @pl.when(where_ref[0] != 0)
    def _():
        numer_into(swap_two_ref, two_ref, out_ref, 0)


def numerators(kernel, count, where, nvir, *blocks):
    share = nvir // NY
    width = blocks[0].shape[1]
    return pl.pallas_call(
        kernel,
        out_shape=jax.ShapeDtypeStruct((NY, count, share, nvir), jnp.float32),
        in_specs=[pl.BlockSpec(memory_space=pltpu.SMEM)] + [pl.BlockSpec(memory_space=pltpu.VMEM)] * len(blocks),
        out_specs=pl.BlockSpec(memory_space=pltpu.VMEM),
        cost_estimate=pl.CostEstimate(
            flops=4 * count * nvir * nvir * width,
            bytes_accessed=2 * len(blocks) * nvir * width + 4 * count * nvir * nvir,
            transcendentals=0,
        ),
        compiler_params=pltpu.CompilerParams(vmem_limit_bytes=24 * 2**20),
    )(where, *blocks)


def local(three_index, occ_energy, vir_energy):
    own = three_index[0]
    nvir, depth = own.shape
    share = nvir // NY
    c, xh, y = lax.axis_index("c"), lax.axis_index("xh"), lax.axis_index("y")

    high = lax.reduce_precision(occ_energy[0], 8, 7)
    rest = occ_energy[0] - high
    middle = lax.reduce_precision(rest, 8, 7)
    line = lax.broadcasted_iota(jnp.int32, (8, 4 * depth), 0)
    tail = jnp.where(line == 0, high, jnp.where(line == 1, middle, jnp.where(line == 2, rest - middle, 0.0)))
    there = across(own)
    beside = other_core(own)
    there, tail = lax.optimization_barrier((there, tail.astype(jnp.bfloat16)))
    there_beside = other_core(there)

    def in_order(first, a, b):
        return jnp.where(first, jnp.concatenate([a, b], axis=1), jnp.concatenate([b, a], axis=1))

    mine = in_order(xh == 0, in_order(c == 0, own, beside), in_order(c == 0, there, there_beside))
    mine = jnp.concatenate([mine, tail], axis=0)

    step_one = moved(
        mine,
        lambda z, xl, xh, y, c: (z - 1, kind(xl, xh), xh, y, c) if c == 0 else (z + 1, xl, xh, y, c),
    )
    beyond = moved(mine, lambda z, xl, xh, y, c: (z, 1 - xl, 1, y, c) if (xh, c) == (0, 0) else None)
    swap_one = other_core(step_one)
    step_two = moved(step_one, lambda z, xl, xh, y, c: (z - 1 if c == 0 else z + 1, xl, xh, y, c))

    def over_y(parts):
        return jnp.sum(lax.all_to_all(parts, "y", 0, 0, tiled=True), axis=0)

    def energy(block):
        terms = block[nvir:, :nvir].astype(jnp.float32)
        return terms[0:1] + terms[1:2] + terms[2:3]

    vir_rows = lax.dynamic_slice_in_dim(vir_energy, y * share, share)
    virs = vir_rows[:, None] + vir_energy[None, :]

    def amps(value, a, b):
        return (value / (virs - a - b)).astype(jnp.bfloat16)

    def by_hops(*parts):
        parts = jnp.stack(parts)
        ahead = [parts] + [moved(parts, lambda z, xl, xh, y, c, n=n: (z, xl, xh, y - n, c)) for n in range(1, NY)]
        twice = jnp.stack(ahead + ahead)
        whole = lax.dynamic_slice_in_dim(twice, NY - y, NY, axis=0)
        return [whole[:, n].reshape(nvir, nvir) for n in range(parts.shape[0])]

    def to_all(*parts):
        parts = jnp.stack(parts)
        whole = lax.all_to_all(jnp.broadcast_to(parts, (NY, *parts.shape)), "y", 0, 0, tiled=True)
        return [whole[:, n].reshape(nvir, nvir) for n in range(parts.shape[0])]

    where = jnp.stack([c, xh])
    parts = numerators(early_kernel, 2, where, nvir, mine, step_one, swap_one, beyond)
    parts, swap_one, step_one_after = lax.optimization_barrier((parts, swap_one, step_one))
    swap_two = moved(swap_one, lambda z, xl, xh, y, c: (z - 1, xl, xh, y, 1) if c == 1 else None)
    turned_one = moved(step_one_after, lambda z, xl, xh, y, c: (z, 1 - xl, 1, y, c) if (xh, c) == (0, 1) else None)
    early = over_y(parts)
    turned_two = moved(step_two, lambda z, xl, xh, y, c: (z, 1 - xl, 1, y, c) if (xh, c) == (0, 1) else None)
    step_three = moved(
        step_two,
        lambda z, xl, xh, y, c: (z - 1, xl, xh, y, c) if c == 0 else (z + 1, kind(xl, xh), xh, y, c),
    )
    turned_four = moved(step_three, lambda z, xl, xh, y, c: (z + 1, xl, xh, y, 1) if c == 1 else None)

    step_two, swap_one, swap_two, early = lax.optimization_barrier((step_two, swap_one, swap_two, early))
    late = over_y(numerators(late_kernel, 1, where, nvir, swap_one, swap_two, step_two))

    mine_energy, one_energy, swap_energy = energy(mine), energy(step_one), energy(swap_one)
    amps_one = amps(
        early[0], jnp.where(c == 0, mine_energy, one_energy), jnp.where(c == 0, one_energy, swap_energy)
    )
    amps_zero = amps(early[1], mine_energy, jnp.where(xh == 0, mine_energy, energy(beyond)))
    first = moved(
        amps_one,
        lambda z, xl, xh, y, c: (z + 1, kind(xl, xh), xh, y, 1) if c == 0 else (z - 1, xl, xh, y, 0),
    )
    second = moved(
        amps_one,
        lambda z, xl, xh, y, c: (z + 1, kind(xl, xh), xh, y, 1) if c == 1 else None,
    )
    second = jnp.where(c == 0, amps_one, second)
    first, second = by_hops(first, second)
    late, first, second, amps_zero, turned_one, turned_two, step_three = lax.optimization_barrier(
        (late, first, second, amps_zero, turned_one, turned_two, step_three)
    )

    amps_two = amps(late[0], jnp.where(c == 0, swap_energy, energy(swap_two)), energy(step_two))
    third = moved(
        amps_two,
        lambda z, xl, xh, y, c: (z - 1, xl, xh, y, 0) if c == 0 else (z - 2, xl, xh, y, 1),
    )
    fourth = moved(amps_two, lambda z, xl, xh, y, c: (z + 2, kind(xl, xh), xh, y, 1) if c == 0 else None)
    fourth = jnp.where(c == 0, amps_zero, fourth)
    third, fourth = to_all(third, fourth)

    def product(dot, *blocks):
        return lambda parts: sum(dot(part, block[:nvir]) for part, block in zip(parts, blocks))

    case = xh * NC + c
    begun = lax.switch(
        case,
        [
            product(dot_nn, step_two, step_one),
            product(dot_tn, step_one, step_two),
            product(dot_nn, step_two, step_one),
            product(dot_tn, turned_one, turned_two),
        ],
        (first, second),
    )

    def ending(h, k, dot, *blocks):
        def branch(parts, total):
            total = total + product(dot, *blocks)(parts)
            cut = [total[:, n * depth : (n + 1) * depth] for n in range(NXH * NC)]
            sent = jnp.concatenate([cut[NC * (1 - h) + 1 - k], cut[NC * h + 1 - k]], axis=1)
            return sent, cut[NC * (1 - h) + k], cut[NC * h + k]

        return branch

    sent, theirs, ours = lax.switch(
        case,
        [
            ending(0, 0, dot_nn, step_three, mine),
            ending(0, 1, dot_tn, turned_four, step_three),
            ending(1, 0, dot_nn, step_three, beyond),
            ending(1, 1, dot_tn, turned_four, step_three),
        ],
        (third, fourth),
        begun,
    )
    got = other_core(sent)
    return (ours + got[:, depth:] + across(theirs + got[:, :depth]))[None]


def solution(mesh):
    grid = Mesh(mesh.devices.reshape(NZ, NXL, NXH, NY, NC), ALL)
    return jax.shard_map(
        local,
        mesh=grid,
        in_specs=(P(("z", "xl"), None, ("xh", "y", "c")), P(("z", "xl")), P()),
        out_specs=P(("z", "xl"), None, ("xh", "y", "c")),
        check_vma=False,
    )
```

```python
import jax
import jax.numpy as jnp
from jax import lax
from jax.experimental import pallas as pl
from jax.experimental.pallas import tpu as pltpu
from jax.sharding import Mesh, PartitionSpec as P

NZ, NXL, NXH, NY, NC = 8, 2, 2, 4, 2
ALL = ("z", "xl", "xh", "y", "c")


def flat(z, xl, xh, y, c):
    return (((z % NZ * NXL + xl % NXL) * NXH + xh % NXH) * NY + y % NY) * NC + c % NC


def moved(array, where):
    pairs = []
    for z in range(NZ):
        for xl in range(NXL):
            for xh in range(NXH):
                for y in range(NY):
                    for c in range(NC):
                        target = where(z, xl, xh, y, c)
                        if target is not None:
                            pairs.append((flat(z, xl, xh, y, c), flat(*target)))
    return lax.ppermute(array, ALL, pairs)


def other_core(array):
    return moved(array, lambda z, xl, xh, y, c: (z, xl, xh, y, 1 - c))


def across(array):
    return moved(array, lambda z, xl, xh, y, c: (z, xl, 1 - xh, y, c))


def kind(xl, xh):
    return xl if xh == 0 else 1 - xl


def dot_nt(a, b):
    return lax.dot_general(a, b, (((1,), (1,)), ((), ())), preferred_element_type=jnp.float32)


def dot_nn(a, b):
    return lax.dot_general(a, b, (((1,), (0,)), ((), ())), preferred_element_type=jnp.float32)


def dot_tn(a, b):
    return lax.dot_general(a, b, (((0,), (0,)), ((), ())), preferred_element_type=jnp.float32)


def numer_into(a_ref, b_ref, out_ref, slot):
    nvir = out_ref.shape[3]
    a, b = a_ref[:nvir, :], b_ref[:nvir, :]
    value = 2.0 * dot_nt(a, b) - dot_nt(b, a)
    out_ref[:, slot] = value.reshape(out_ref.shape[0], out_ref.shape[2], nvir)


def early_kernel(where_ref, mine_ref, one_ref, swap_ref, beyond_ref, out_ref):
    @pl.when(where_ref[0] == 0)
    def _():
        numer_into(mine_ref, one_ref, out_ref, 0)

    @pl.when(where_ref[0] != 0)
    def _():
        numer_into(one_ref, swap_ref, out_ref, 0)

    @pl.when(where_ref[1] == 0)
    def _():
        numer_into(mine_ref, mine_ref, out_ref, 1)

    @pl.when(where_ref[1] != 0)
    def _():
        numer_into(mine_ref, beyond_ref, out_ref, 1)


def late_kernel(where_ref, swap_one_ref, swap_two_ref, two_ref, out_ref):
    @pl.when(where_ref[0] == 0)
    def _():
        numer_into(swap_one_ref, two_ref, out_ref, 0)

    @pl.when(where_ref[0] != 0)
    def _():
        numer_into(swap_two_ref, two_ref, out_ref, 0)


def numerators(kernel, count, where, nvir, *blocks):
    share = nvir // NY
    width = blocks[0].shape[1]
    return pl.pallas_call(
        kernel,
        out_shape=jax.ShapeDtypeStruct((NY, count, share, nvir), jnp.float32),
        in_specs=[pl.BlockSpec(memory_space=pltpu.SMEM)] + [pl.BlockSpec(memory_space=pltpu.VMEM)] * len(blocks),
        out_specs=pl.BlockSpec(memory_space=pltpu.VMEM),
        cost_estimate=pl.CostEstimate(
            flops=4 * count * nvir * nvir * width,
            bytes_accessed=2 * len(blocks) * nvir * width + 4 * count * nvir * nvir,
            transcendentals=0,
        ),
        compiler_params=pltpu.CompilerParams(vmem_limit_bytes=24 * 2**20),
    )(where, *blocks)


def local(three_index, occ_energy, vir_energy):
    own = three_index[0]
    nvir, depth = own.shape
    share = nvir // NY
    c, xh, y = lax.axis_index("c"), lax.axis_index("xh"), lax.axis_index("y")

    high = lax.reduce_precision(occ_energy[0], 8, 7)
    rest = occ_energy[0] - high
    middle = lax.reduce_precision(rest, 8, 7)
    line = lax.broadcasted_iota(jnp.int32, (8, 4 * depth), 0)
    tail = jnp.where(line == 0, high, jnp.where(line == 1, middle, jnp.where(line == 2, rest - middle, 0.0)))
    there = across(own)
    beside = other_core(own)
    there, tail = lax.optimization_barrier((there, tail.astype(jnp.bfloat16)))
    there_beside = other_core(there)

    def in_order(first, a, b):
        return jnp.where(first, jnp.concatenate([a, b], axis=1), jnp.concatenate([b, a], axis=1))

    mine = in_order(xh == 0, in_order(c == 0, own, beside), in_order(c == 0, there, there_beside))
    mine = jnp.concatenate([mine, tail], axis=0)

    step_one = moved(
        mine,
        lambda z, xl, xh, y, c: (z - 1, kind(xl, xh), xh, y, c) if c == 0 else (z + 1, xl, xh, y, c),
    )
    beyond = moved(mine, lambda z, xl, xh, y, c: (z, 1 - xl, 1, y, c) if (xh, c) == (0, 0) else None)
    swap_one = other_core(step_one)
    step_two = moved(step_one, lambda z, xl, xh, y, c: (z - 1 if c == 0 else z + 1, xl, xh, y, c))

    def exchanged(parts):
        return lax.all_to_all(parts, "y", 0, 0, tiled=True)

    def energy(block):
        terms = block[nvir:, :nvir].astype(jnp.float32)
        return terms[0:1] + terms[1:2] + terms[2:3]

    vir_rows = lax.dynamic_slice_in_dim(vir_energy, y * share, share)
    virs = vir_rows[:, None] + vir_energy[None, :]

    def amps(value, a, b):
        return (value / (virs - a - b)).astype(jnp.bfloat16)

    def to_all(*parts):
        parts = jnp.stack(parts)
        whole = lax.all_to_all(jnp.broadcast_to(parts, (NY, *parts.shape)), "y", 0, 0, tiled=True)
        return [whole[:, n].reshape(nvir, nvir) for n in range(parts.shape[0])]

    where = jnp.stack([c, xh])
    parts = numerators(early_kernel, 2, where, nvir, mine, step_one, swap_one, beyond)
    parts, swap_one, step_one_after = lax.optimization_barrier((parts, swap_one, step_one))
    swap_two = moved(swap_one, lambda z, xl, xh, y, c: (z - 1, xl, xh, y, 1) if c == 1 else None)
    turned_one = moved(step_one_after, lambda z, xl, xh, y, c: (z, 1 - xl, 1, y, c) if (xh, c) == (0, 1) else None)
    early = exchanged(parts)
    turned_two = moved(step_two, lambda z, xl, xh, y, c: (z, 1 - xl, 1, y, c) if (xh, c) == (0, 1) else None)
    step_three = moved(
        step_two,
        lambda z, xl, xh, y, c: (z - 1, xl, xh, y, c) if c == 0 else (z + 1, kind(xl, xh), xh, y, c),
    )
    turned_four = moved(step_three, lambda z, xl, xh, y, c: (z + 1, xl, xh, y, 1) if c == 1 else None)

    parts = numerators(late_kernel, 1, where, nvir, swap_one, swap_two, step_two)
    early, parts = lax.optimization_barrier((early, parts))
    early, late = jnp.sum(early, axis=0), jnp.sum(exchanged(parts), axis=0)

    mine_energy, one_energy, swap_energy = energy(mine), energy(step_one), energy(swap_one)
    amps_one = amps(
        early[0], jnp.where(c == 0, mine_energy, one_energy), jnp.where(c == 0, one_energy, swap_energy)
    )
    amps_zero = amps(early[1], mine_energy, jnp.where(xh == 0, mine_energy, energy(beyond)))
    first = moved(
        amps_one,
        lambda z, xl, xh, y, c: (z + 1, kind(xl, xh), xh, y, 1) if c == 0 else (z - 1, xl, xh, y, 0),
    )
    second = moved(
        amps_one,
        lambda z, xl, xh, y, c: (z + 1, kind(xl, xh), xh, y, 1) if c == 1 else None,
    )
    second = jnp.where(c == 0, amps_one, second)
    late, first, second, amps_zero, turned_one, turned_two, step_three = lax.optimization_barrier(
        (late, first, second, amps_zero, turned_one, turned_two, step_three)
    )

    first, second = to_all(first, second)

    amps_two = amps(late[0], jnp.where(c == 0, swap_energy, energy(swap_two)), energy(step_two))
    third = moved(
        amps_two,
        lambda z, xl, xh, y, c: (z - 1, xl, xh, y, 0) if c == 0 else (z - 2, xl, xh, y, 1),
    )
    fourth = moved(amps_two, lambda z, xl, xh, y, c: (z + 2, kind(xl, xh), xh, y, 1) if c == 0 else None)
    fourth = jnp.where(c == 0, amps_zero, fourth)
    third, fourth, first, second, turned_two = lax.optimization_barrier((third, fourth, first, second, turned_two))
    third, fourth = to_all(third, fourth)

    def product(dot, *blocks):
        return lambda parts: sum(dot(part, block[:nvir]) for part, block in zip(parts, blocks))

    case = xh * NC + c
    begun = lax.switch(
        case,
        [
            product(dot_nn, step_two, step_one),
            product(dot_tn, step_one, step_two),
            product(dot_nn, step_two, step_one),
            product(dot_tn, turned_one, turned_two),
        ],
        (first, second),
    )

    def ending(h, k, dot, *blocks):
        def branch(parts, total):
            total = total + product(dot, *blocks)(parts)
            cut = [total[:, n * depth : (n + 1) * depth] for n in range(NXH * NC)]
            sent = jnp.concatenate([cut[NC * (1 - h) + 1 - k], cut[NC * h + 1 - k]], axis=1)
            return sent, cut[NC * (1 - h) + k], cut[NC * h + k]

        return branch

    sent, theirs, ours = lax.switch(
        case,
        [
            ending(0, 0, dot_nn, step_three, mine),
            ending(0, 1, dot_tn, turned_four, step_three),
            ending(1, 0, dot_nn, step_three, beyond),
            ending(1, 1, dot_tn, turned_four, step_three),
        ],
        (third, fourth),
        begun,
    )
    got = other_core(sent)
    return (ours + got[:, depth:] + across(theirs + got[:, :depth]))[None]


def solution(mesh):
    grid = Mesh(mesh.devices.reshape(NZ, NXL, NXH, NY, NC), ALL)
    return jax.shard_map(
        local,
        mesh=grid,
        in_specs=(P(("z", "xl"), None, ("xh", "y", "c")), P(("z", "xl")), P()),
        out_specs=P(("z", "xl"), None, ("xh", "y", "c")),
        check_vma=False,
    )
```

```python
import jax
import jax.numpy as jnp
from jax import lax
from jax.experimental import pallas as pl
from jax.experimental.pallas import tpu as pltpu
from jax.sharding import Mesh, PartitionSpec as P

NZ, NXL, NXH, NY, NC = 8, 2, 2, 4, 2
ALL = ("z", "xl", "xh", "y", "c")


def flat(z, xl, xh, y, c):
    return (((z % NZ * NXL + xl % NXL) * NXH + xh % NXH) * NY + y % NY) * NC + c % NC


def moved(array, where):
    pairs = []
    for z in range(NZ):
        for xl in range(NXL):
            for xh in range(NXH):
                for y in range(NY):
                    for c in range(NC):
                        target = where(z, xl, xh, y, c)
                        if target is not None:
                            pairs.append((flat(z, xl, xh, y, c), flat(*target)))
    return lax.ppermute(array, ALL, pairs)


def other_core(array):
    return moved(array, lambda z, xl, xh, y, c: (z, xl, xh, y, 1 - c))


def across(array):
    return moved(array, lambda z, xl, xh, y, c: (z, xl, 1 - xh, y, c))


def kind(xl, xh):
    return xl if xh == 0 else 1 - xl


def dot_nt(a, b):
    return lax.dot_general(a, b, (((1,), (1,)), ((), ())), preferred_element_type=jnp.float32)


def dot_nn(a, b):
    return lax.dot_general(a, b, (((1,), (0,)), ((), ())), preferred_element_type=jnp.float32)


def dot_tn(a, b):
    return lax.dot_general(a, b, (((0,), (0,)), ((), ())), preferred_element_type=jnp.float32)


def numer_into(a_ref, b_ref, out_ref, slot):
    nvir = out_ref.shape[3]
    a, b = a_ref[:nvir, :], b_ref[:nvir, :]
    value = 2.0 * dot_nt(a, b) - dot_nt(b, a)
    out_ref[:, slot] = value.reshape(out_ref.shape[0], out_ref.shape[2], nvir)


def early_kernel(where_ref, mine_ref, one_ref, swap_ref, beyond_ref, out_ref):
    @pl.when(where_ref[0] == 0)
    def _():
        numer_into(mine_ref, one_ref, out_ref, 0)

    @pl.when(where_ref[0] != 0)
    def _():
        numer_into(one_ref, swap_ref, out_ref, 0)

    @pl.when(where_ref[1] == 0)
    def _():
        numer_into(mine_ref, mine_ref, out_ref, 1)

    @pl.when(where_ref[1] != 0)
    def _():
        numer_into(mine_ref, beyond_ref, out_ref, 1)


def late_kernel(where_ref, swap_one_ref, swap_two_ref, two_ref, out_ref):
    @pl.when(where_ref[0] == 0)
    def _():
        numer_into(swap_one_ref, two_ref, out_ref, 0)

    @pl.when(where_ref[0] != 0)
    def _():
        numer_into(swap_two_ref, two_ref, out_ref, 0)


def numerators(kernel, count, where, nvir, *blocks):
    share = nvir // NY
    width = blocks[0].shape[1]
    return pl.pallas_call(
        kernel,
        out_shape=jax.ShapeDtypeStruct((NY, count, share, nvir), jnp.float32),
        in_specs=[pl.BlockSpec(memory_space=pltpu.SMEM)] + [pl.BlockSpec(memory_space=pltpu.VMEM)] * len(blocks),
        out_specs=pl.BlockSpec(memory_space=pltpu.VMEM),
        cost_estimate=pl.CostEstimate(
            flops=4 * count * nvir * nvir * width,
            bytes_accessed=2 * len(blocks) * nvir * width + 4 * count * nvir * nvir,
            transcendentals=0,
        ),
        compiler_params=pltpu.CompilerParams(vmem_limit_bytes=24 * 2**20),
    )(where, *blocks)


def local(three_index, occ_energy, vir_energy):
    own = three_index[0]
    nvir, depth = own.shape
    share = nvir // NY
    c, xh, y = lax.axis_index("c"), lax.axis_index("xh"), lax.axis_index("y")

    high = lax.reduce_precision(occ_energy[0], 8, 7)
    rest = occ_energy[0] - high
    middle = lax.reduce_precision(rest, 8, 7)
    line = lax.broadcasted_iota(jnp.int32, (8, 4 * depth), 0)
    tail = jnp.where(line == 0, high, jnp.where(line == 1, middle, jnp.where(line == 2, rest - middle, 0.0)))
    there = across(own)
    beside = other_core(own)
    there, tail = lax.optimization_barrier((there, tail.astype(jnp.bfloat16)))
    there_beside = other_core(there)

    def in_order(first, a, b):
        return jnp.where(first, jnp.concatenate([a, b], axis=1), jnp.concatenate([b, a], axis=1))

    mine = in_order(xh == 0, in_order(c == 0, own, beside), in_order(c == 0, there, there_beside))
    mine = jnp.concatenate([mine, tail], axis=0)

    step_one = moved(
        mine,
        lambda z, xl, xh, y, c: (z - 1, kind(xl, xh), xh, y, c) if c == 0 else (z + 1, xl, xh, y, c),
    )
    beyond = moved(mine, lambda z, xl, xh, y, c: (z, 1 - xl, 1, y, c) if (xh, c) == (0, 0) else None)
    swap_one = other_core(step_one)
    step_two = moved(step_one, lambda z, xl, xh, y, c: (z - 1 if c == 0 else z + 1, xl, xh, y, c))

    def exchanged(parts):
        return lax.all_to_all(parts, "y", 0, 0, tiled=True)

    def energy(block):
        terms = block[nvir:, :nvir].astype(jnp.float32)
        return terms[0:1] + terms[1:2] + terms[2:3]

    vir_rows = lax.dynamic_slice_in_dim(vir_energy, y * share, share)
    virs = vir_rows[:, None] + vir_energy[None, :]

    def amps(value, a, b):
        return (value / (virs - a - b)).astype(jnp.bfloat16)

    def by_hops(*parts):
        parts = jnp.stack(parts)
        hops = [parts] + [moved(parts, lambda z, xl, xh, y, c, n=n: (z, xl, xh, y - n, c)) for n in range(1, NY)]
        whole = lax.dynamic_slice_in_dim(jnp.stack(hops + hops[:-1]), (NY - y) % NY, NY, axis=0)
        return [whole[:, n].reshape(nvir, nvir) for n in range(parts.shape[0])]

    def to_all(*parts):
        parts = jnp.stack(parts)
        whole = lax.all_to_all(jnp.broadcast_to(parts, (NY, *parts.shape)), "y", 0, 0, tiled=True)
        return [whole[:, n].reshape(nvir, nvir) for n in range(parts.shape[0])]

    where = jnp.stack([c, xh])
    parts = numerators(early_kernel, 2, where, nvir, mine, step_one, swap_one, beyond)
    parts, swap_one, step_one_after = lax.optimization_barrier((parts, swap_one, step_one))
    swap_two = moved(swap_one, lambda z, xl, xh, y, c: (z - 1, xl, xh, y, 1) if c == 1 else None)
    turned_one = moved(step_one_after, lambda z, xl, xh, y, c: (z, 1 - xl, 1, y, c) if (xh, c) == (0, 1) else None)
    early = exchanged(parts)
    turned_two = moved(step_two, lambda z, xl, xh, y, c: (z, 1 - xl, 1, y, c) if (xh, c) == (0, 1) else None)
    step_three = moved(
        step_two,
        lambda z, xl, xh, y, c: (z - 1, xl, xh, y, c) if c == 0 else (z + 1, kind(xl, xh), xh, y, c),
    )
    turned_four = moved(step_three, lambda z, xl, xh, y, c: (z + 1, xl, xh, y, 1) if c == 1 else None)

    parts = numerators(late_kernel, 1, where, nvir, swap_one, swap_two, step_two)
    early, parts = lax.optimization_barrier((early, parts))
    early, late = jnp.sum(early, axis=0), jnp.sum(exchanged(parts), axis=0)

    mine_energy, one_energy, swap_energy = energy(mine), energy(step_one), energy(swap_one)
    amps_one = amps(
        early[0], jnp.where(c == 0, mine_energy, one_energy), jnp.where(c == 0, one_energy, swap_energy)
    )
    amps_zero = amps(early[1], mine_energy, jnp.where(xh == 0, mine_energy, energy(beyond)))
    first = moved(
        amps_one,
        lambda z, xl, xh, y, c: (z + 1, kind(xl, xh), xh, y, 1) if c == 0 else (z - 1, xl, xh, y, 0),
    )
    second = moved(
        amps_one,
        lambda z, xl, xh, y, c: (z + 1, kind(xl, xh), xh, y, 1) if c == 1 else None,
    )
    second = jnp.where(c == 0, amps_one, second)
    late, first, second, amps_zero, turned_one, turned_two, step_three = lax.optimization_barrier(
        (late, first, second, amps_zero, turned_one, turned_two, step_three)
    )

    first, second = to_all(first, second)

    amps_two = amps(late[0], jnp.where(c == 0, swap_energy, energy(swap_two)), energy(step_two))
    third = moved(
        amps_two,
        lambda z, xl, xh, y, c: (z - 1, xl, xh, y, 0) if c == 0 else (z - 2, xl, xh, y, 1),
    )
    fourth = moved(amps_two, lambda z, xl, xh, y, c: (z + 2, kind(xl, xh), xh, y, 1) if c == 0 else None)
    fourth = jnp.where(c == 0, amps_zero, fourth)
    third, fourth, first, second, turned_two = lax.optimization_barrier((third, fourth, first, second, turned_two))
    third, fourth = by_hops(third, fourth)

    def product(dot, *blocks):
        return lambda parts: sum(dot(part, block[:nvir]) for part, block in zip(parts, blocks))

    case = xh * NC + c
    begun = lax.switch(
        case,
        [
            product(dot_nn, step_two, step_one),
            product(dot_tn, step_one, step_two),
            product(dot_nn, step_two, step_one),
            product(dot_tn, turned_one, turned_two),
        ],
        (first, second),
    )

    def ending(h, k, dot, *blocks):
        def branch(parts, total):
            total = total + product(dot, *blocks)(parts)
            cut = [total[:, n * depth : (n + 1) * depth] for n in range(NXH * NC)]
            sent = jnp.concatenate([cut[NC * (1 - h) + 1 - k], cut[NC * h + 1 - k]], axis=1)
            return sent, cut[NC * (1 - h) + k], cut[NC * h + k]

        return branch

    sent, theirs, ours = lax.switch(
        case,
        [
            ending(0, 0, dot_nn, step_three, mine),
            ending(0, 1, dot_tn, turned_four, step_three),
            ending(1, 0, dot_nn, step_three, beyond),
            ending(1, 1, dot_tn, turned_four, step_three),
        ],
        (third, fourth),
        begun,
    )
    got = other_core(sent)
    return (ours + got[:, depth:] + across(theirs + got[:, :depth]))[None]


def solution(mesh):
    grid = Mesh(mesh.devices.reshape(NZ, NXL, NXH, NY, NC), ALL)
    return jax.shard_map(
        local,
        mesh=grid,
        in_specs=(P(("z", "xl"), None, ("xh", "y", "c")), P(("z", "xl")), P()),
        out_specs=P(("z", "xl"), None, ("xh", "y", "c")),
        check_vma=False,
    )
```

```python
import jax
import jax.numpy as jnp
from jax import lax
from jax.experimental import pallas as pl
from jax.experimental.pallas import tpu as pltpu
from jax.sharding import Mesh, PartitionSpec as P

NZ, NXL, NXH, NY, NC = 8, 2, 2, 4, 2
ALL = ("z", "xl", "xh", "y", "c")


def flat(z, xl, xh, y, c):
    return (((z % NZ * NXL + xl % NXL) * NXH + xh % NXH) * NY + y % NY) * NC + c % NC


def moved(array, where):
    pairs = []
    for z in range(NZ):
        for xl in range(NXL):
            for xh in range(NXH):
                for y in range(NY):
                    for c in range(NC):
                        target = where(z, xl, xh, y, c)
                        if target is not None:
                            pairs.append((flat(z, xl, xh, y, c), flat(*target)))
    return lax.ppermute(array, ALL, pairs)


def other_core(array):
    return moved(array, lambda z, xl, xh, y, c: (z, xl, xh, y, 1 - c))


def across(array):
    return moved(array, lambda z, xl, xh, y, c: (z, xl, 1 - xh, y, c))


def kind(xl, xh):
    return xl if xh == 0 else 1 - xl


def dot_nt(a, b):
    return lax.dot_general(a, b, (((1,), (1,)), ((), ())), preferred_element_type=jnp.float32)


def dot_nn(a, b):
    return lax.dot_general(a, b, (((1,), (0,)), ((), ())), preferred_element_type=jnp.float32)


def dot_tn(a, b):
    return lax.dot_general(a, b, (((0,), (0,)), ((), ())), preferred_element_type=jnp.float32)


def numer_into(a_ref, b_ref, out_ref, slot):
    nvir = out_ref.shape[3]
    a, b = a_ref[:nvir, :], b_ref[:nvir, :]
    value = 2.0 * dot_nt(a, b) - dot_nt(b, a)
    out_ref[:, slot] = value.reshape(out_ref.shape[0], out_ref.shape[2], nvir)


def early_kernel(where_ref, mine_ref, one_ref, swap_ref, beyond_ref, out_ref):
    @pl.when(where_ref[0] == 0)
    def _():
        numer_into(mine_ref, one_ref, out_ref, 0)

    @pl.when(where_ref[0] != 0)
    def _():
        numer_into(one_ref, swap_ref, out_ref, 0)

    @pl.when(where_ref[1] == 0)
    def _():
        numer_into(mine_ref, mine_ref, out_ref, 1)

    @pl.when(where_ref[1] != 0)
    def _():
        numer_into(mine_ref, beyond_ref, out_ref, 1)


def late_kernel(where_ref, swap_one_ref, swap_two_ref, two_ref, out_ref):
    @pl.when(where_ref[0] == 0)
    def _():
        numer_into(swap_one_ref, two_ref, out_ref, 0)

    @pl.when(where_ref[0] != 0)
    def _():
        numer_into(swap_two_ref, two_ref, out_ref, 0)


def numerators(kernel, count, where, nvir, *blocks):
    share = nvir // NY
    width = blocks[0].shape[1]
    return pl.pallas_call(
        kernel,
        out_shape=jax.ShapeDtypeStruct((NY, count, share, nvir), jnp.float32),
        in_specs=[pl.BlockSpec(memory_space=pltpu.SMEM)] + [pl.BlockSpec(memory_space=pltpu.VMEM)] * len(blocks),
        out_specs=pl.BlockSpec(memory_space=pltpu.VMEM),
        cost_estimate=pl.CostEstimate(
            flops=4 * count * nvir * nvir * width,
            bytes_accessed=2 * len(blocks) * nvir * width + 4 * count * nvir * nvir,
            transcendentals=0,
        ),
        compiler_params=pltpu.CompilerParams(vmem_limit_bytes=24 * 2**20),
    )(where, *blocks)


def local(three_index, occ_energy, vir_energy):
    own = three_index[0]
    nvir, depth = own.shape
    share = nvir // NY
    c, xh, y = lax.axis_index("c"), lax.axis_index("xh"), lax.axis_index("y")

    high = lax.reduce_precision(occ_energy[0], 8, 7)
    rest = occ_energy[0] - high
    middle = lax.reduce_precision(rest, 8, 7)
    line = lax.broadcasted_iota(jnp.int32, (8, 4 * depth), 0)
    tail = jnp.where(line == 0, high, jnp.where(line == 1, middle, jnp.where(line == 2, rest - middle, 0.0)))
    there = across(own)
    beside = other_core(own)
    there, tail = lax.optimization_barrier((there, tail.astype(jnp.bfloat16)))
    there_beside = other_core(there)

    def in_order(first, a, b):
        return jnp.where(first, jnp.concatenate([a, b], axis=1), jnp.concatenate([b, a], axis=1))

    mine = in_order(xh == 0, in_order(c == 0, own, beside), in_order(c == 0, there, there_beside))
    mine = jnp.concatenate([mine, tail], axis=0)

    step_one = moved(
        mine,
        lambda z, xl, xh, y, c: (z - 1, kind(xl, xh), xh, y, c) if c == 0 else (z + 1, xl, xh, y, c),
    )
    beyond = moved(mine, lambda z, xl, xh, y, c: (z, 1 - xl, 1, y, c) if (xh, c) == (0, 0) else None)
    swap_one = other_core(step_one)
    step_two = moved(step_one, lambda z, xl, xh, y, c: (z - 1 if c == 0 else z + 1, xl, xh, y, c))

    def exchanged(parts):
        return lax.all_to_all(parts, "y", 0, 0, tiled=True)

    def energy(block):
        terms = block[nvir:, :nvir].astype(jnp.float32)
        return terms[0:1] + terms[1:2] + terms[2:3]

    vir_rows = lax.dynamic_slice_in_dim(vir_energy, y * share, share)
    virs = vir_rows[:, None] + vir_energy[None, :]

    def amps(value, a, b):
        return (value / (virs - a - b)).astype(jnp.bfloat16)

    def by_hops(*parts):
        parts = jnp.stack(parts)
        hops = [parts] + [moved(parts, lambda z, xl, xh, y, c, n=n: (z, xl, xh, y - n, c)) for n in range(1, NY)]
        return [
            jnp.concatenate([lax.select_n(y, *(hops[(k - n) % NY][m] for n in range(NY))) for k in range(NY)], axis=0)
            for m in range(parts.shape[0])
        ]

    def to_all(*parts):
        parts = jnp.stack(parts)
        whole = lax.all_to_all(jnp.broadcast_to(parts, (NY, *parts.shape)), "y", 0, 0, tiled=True)
        return [whole[:, n].reshape(nvir, nvir) for n in range(parts.shape[0])]

    where = jnp.stack([c, xh])
    parts = numerators(early_kernel, 2, where, nvir, mine, step_one, swap_one, beyond)
    parts, swap_one, step_one_after = lax.optimization_barrier((parts, swap_one, step_one))
    swap_two = moved(swap_one, lambda z, xl, xh, y, c: (z - 1, xl, xh, y, 1) if c == 1 else None)
    turned_one = moved(step_one_after, lambda z, xl, xh, y, c: (z, 1 - xl, 1, y, c) if (xh, c) == (0, 1) else None)
    early = exchanged(parts)
    turned_two = moved(step_two, lambda z, xl, xh, y, c: (z, 1 - xl, 1, y, c) if (xh, c) == (0, 1) else None)
    step_three = moved(
        step_two,
        lambda z, xl, xh, y, c: (z - 1, xl, xh, y, c) if c == 0 else (z + 1, kind(xl, xh), xh, y, c),
    )
    turned_four = moved(step_three, lambda z, xl, xh, y, c: (z + 1, xl, xh, y, 1) if c == 1 else None)

    parts = numerators(late_kernel, 1, where, nvir, swap_one, swap_two, step_two)
    early, parts = lax.optimization_barrier((early, parts))
    early, late = jnp.sum(early, axis=0), jnp.sum(exchanged(parts), axis=0)

    mine_energy, one_energy, swap_energy = energy(mine), energy(step_one), energy(swap_one)
    amps_one = amps(
        early[0], jnp.where(c == 0, mine_energy, one_energy), jnp.where(c == 0, one_energy, swap_energy)
    )
    amps_zero = amps(early[1], mine_energy, jnp.where(xh == 0, mine_energy, energy(beyond)))
    first = moved(
        amps_one,
        lambda z, xl, xh, y, c: (z + 1, kind(xl, xh), xh, y, 1) if c == 0 else (z - 1, xl, xh, y, 0),
    )
    second = moved(
        amps_one,
        lambda z, xl, xh, y, c: (z + 1, kind(xl, xh), xh, y, 1) if c == 1 else None,
    )
    second = jnp.where(c == 0, amps_one, second)
    late, first, second, amps_zero, turned_one, turned_two, step_three = lax.optimization_barrier(
        (late, first, second, amps_zero, turned_one, turned_two, step_three)
    )

    first, second = to_all(first, second)

    amps_two = amps(late[0], jnp.where(c == 0, swap_energy, energy(swap_two)), energy(step_two))
    third = moved(
        amps_two,
        lambda z, xl, xh, y, c: (z - 1, xl, xh, y, 0) if c == 0 else (z - 2, xl, xh, y, 1),
    )
    fourth = moved(amps_two, lambda z, xl, xh, y, c: (z + 2, kind(xl, xh), xh, y, 1) if c == 0 else None)
    fourth = jnp.where(c == 0, amps_zero, fourth)
    third, fourth, first, second, turned_two = lax.optimization_barrier((third, fourth, first, second, turned_two))
    third, fourth = by_hops(third, fourth)

    def product(dot, *blocks):
        return lambda parts: sum(dot(part, block[:nvir]) for part, block in zip(parts, blocks))

    case = xh * NC + c
    begun = lax.switch(
        case,
        [
            product(dot_nn, step_two, step_one),
            product(dot_tn, step_one, step_two),
            product(dot_nn, step_two, step_one),
            product(dot_tn, turned_one, turned_two),
        ],
        (first, second),
    )

    def ending(h, k, dot, *blocks):
        def branch(parts, total):
            total = total + product(dot, *blocks)(parts)
            cut = [total[:, n * depth : (n + 1) * depth] for n in range(NXH * NC)]
            sent = jnp.concatenate([cut[NC * (1 - h) + 1 - k], cut[NC * h + 1 - k]], axis=1)
            return sent, cut[NC * (1 - h) + k], cut[NC * h + k]

        return branch

    sent, theirs, ours = lax.switch(
        case,
        [
            ending(0, 0, dot_nn, step_three, mine),
            ending(0, 1, dot_tn, turned_four, step_three),
            ending(1, 0, dot_nn, step_three, beyond),
            ending(1, 1, dot_tn, turned_four, step_three),
        ],
        (third, fourth),
        begun,
    )
    got = other_core(sent)
    return (ours + got[:, depth:] + across(theirs + got[:, :depth]))[None]


def solution(mesh):
    grid = Mesh(mesh.devices.reshape(NZ, NXL, NXH, NY, NC), ALL)
    return jax.shard_map(
        local,
        mesh=grid,
        in_specs=(P(("z", "xl"), None, ("xh", "y", "c")), P(("z", "xl")), P()),
        out_specs=P(("z", "xl"), None, ("xh", "y", "c")),
        check_vma=False,
    )
```

```python
import jax
import jax.numpy as jnp
from jax import lax
from jax.experimental import pallas as pl
from jax.experimental.pallas import tpu as pltpu
from jax.sharding import Mesh, PartitionSpec as P

NZ, NXL, NXH, NY, NC = 8, 2, 2, 4, 2
ALL = ("z", "xl", "xh", "y", "c")


def flat(z, xl, xh, y, c):
    return (((z % NZ * NXL + xl % NXL) * NXH + xh % NXH) * NY + y % NY) * NC + c % NC


def moved(array, where):
    pairs = []
    for z in range(NZ):
        for xl in range(NXL):
            for xh in range(NXH):
                for y in range(NY):
                    for c in range(NC):
                        target = where(z, xl, xh, y, c)
                        if target is not None:
                            pairs.append((flat(z, xl, xh, y, c), flat(*target)))
    return lax.ppermute(array, ALL, pairs)


def other_core(array):
    return moved(array, lambda z, xl, xh, y, c: (z, xl, xh, y, 1 - c))


def across(array):
    return moved(array, lambda z, xl, xh, y, c: (z, xl, 1 - xh, y, c))


def kind(xl, xh):
    return xl if xh == 0 else 1 - xl


def dot_nt(a, b):
    return lax.dot_general(a, b, (((1,), (1,)), ((), ())), preferred_element_type=jnp.float32)


def dot_nn(a, b):
    return lax.dot_general(a, b, (((1,), (0,)), ((), ())), preferred_element_type=jnp.float32)


def dot_tn(a, b):
    return lax.dot_general(a, b, (((0,), (0,)), ((), ())), preferred_element_type=jnp.float32)


def numer_into(a_ref, b_ref, out_ref, slot):
    nvir = out_ref.shape[3]
    a, b = a_ref[:nvir, :], b_ref[:nvir, :]
    value = 2.0 * dot_nt(a, b) - dot_nt(b, a)
    out_ref[:, slot] = value.reshape(out_ref.shape[0], out_ref.shape[2], nvir)


def early_kernel(where_ref, mine_ref, one_ref, swap_ref, beyond_ref, out_ref):
    @pl.when(where_ref[0] == 0)
    def _():
        numer_into(mine_ref, one_ref, out_ref, 0)

    @pl.when(where_ref[0] != 0)
    def _():
        numer_into(one_ref, swap_ref, out_ref, 0)

    @pl.when(where_ref[1] == 0)
    def _():
        numer_into(mine_ref, mine_ref, out_ref, 1)

    @pl.when(where_ref[1] != 0)
    def _():
        numer_into(mine_ref, beyond_ref, out_ref, 1)


def late_kernel(where_ref, swap_one_ref, swap_two_ref, two_ref, out_ref):
    @pl.when(where_ref[0] == 0)
    def _():
        numer_into(swap_one_ref, two_ref, out_ref, 0)

    @pl.when(where_ref[0] != 0)
    def _():
        numer_into(swap_two_ref, two_ref, out_ref, 0)


def numerators(kernel, count, where, nvir, *blocks):
    share = nvir // NY
    width = blocks[0].shape[1]
    return pl.pallas_call(
        kernel,
        out_shape=jax.ShapeDtypeStruct((NY, count, share, nvir), jnp.float32),
        in_specs=[pl.BlockSpec(memory_space=pltpu.SMEM)] + [pl.BlockSpec(memory_space=pltpu.VMEM)] * len(blocks),
        out_specs=pl.BlockSpec(memory_space=pltpu.VMEM),
        cost_estimate=pl.CostEstimate(
            flops=4 * count * nvir * nvir * width,
            bytes_accessed=2 * len(blocks) * nvir * width + 4 * count * nvir * nvir,
            transcendentals=0,
        ),
        compiler_params=pltpu.CompilerParams(vmem_limit_bytes=24 * 2**20),
    )(where, *blocks)


def local(three_index, occ_energy, vir_energy):
    own = three_index[0]
    nvir, depth = own.shape
    share = nvir // NY
    c, xh, y = lax.axis_index("c"), lax.axis_index("xh"), lax.axis_index("y")

    high = lax.reduce_precision(occ_energy[0], 8, 7)
    rest = occ_energy[0] - high
    middle = lax.reduce_precision(rest, 8, 7)
    line = lax.broadcasted_iota(jnp.int32, (8, 4 * depth), 0)
    tail = jnp.where(line == 0, high, jnp.where(line == 1, middle, jnp.where(line == 2, rest - middle, 0.0)))
    there = across(own)
    beside = other_core(own)
    there, tail = lax.optimization_barrier((there, tail.astype(jnp.bfloat16)))
    there_beside = other_core(there)

    def in_order(first, a, b):
        return jnp.where(first, jnp.concatenate([a, b], axis=1), jnp.concatenate([b, a], axis=1))

    mine = in_order(xh == 0, in_order(c == 0, own, beside), in_order(c == 0, there, there_beside))
    mine = jnp.concatenate([mine, tail], axis=0)

    step_one = moved(
        mine,
        lambda z, xl, xh, y, c: (z - 1, kind(xl, xh), xh, y, c) if c == 0 else (z + 1, xl, xh, y, c),
    )
    beyond = moved(mine, lambda z, xl, xh, y, c: (z, 1 - xl, 1, y, c) if (xh, c) == (0, 0) else None)
    swap_one = other_core(step_one)
    step_two = moved(step_one, lambda z, xl, xh, y, c: (z - 1 if c == 0 else z + 1, xl, xh, y, c))

    def exchanged(parts):
        return lax.all_to_all(parts, "y", 0, 0, tiled=True)

    def energy(block):
        terms = block[nvir:, :nvir].astype(jnp.float32)
        return terms[0:1] + terms[1:2] + terms[2:3]

    vir_rows = lax.dynamic_slice_in_dim(vir_energy, y * share, share)
    virs = vir_rows[:, None] + vir_energy[None, :]

    def amps(value, a, b):
        return (value / (virs - a - b)).astype(jnp.bfloat16)

    def by_hops(*parts):
        parts = jnp.stack(parts)
        hops = [parts] + [moved(parts, lambda z, xl, xh, y, c, n=n: (z, xl, xh, y - n, c)) for n in range(1, NY)]
        return [
            jnp.concatenate([lax.select_n(y, *(hops[(k - n) % NY][m] for n in range(NY))) for k in range(NY)], axis=0)
            for m in range(parts.shape[0])
        ]

    where = jnp.stack([c, xh])
    parts = numerators(early_kernel, 2, where, nvir, mine, step_one, swap_one, beyond)
    parts, swap_one, step_one_after = lax.optimization_barrier((parts, swap_one, step_one))
    swap_two = moved(swap_one, lambda z, xl, xh, y, c: (z - 1, xl, xh, y, 1) if c == 1 else None)
    turned_one = moved(step_one_after, lambda z, xl, xh, y, c: (z, 1 - xl, 1, y, c) if (xh, c) == (0, 1) else None)
    early = exchanged(parts)
    turned_two = moved(step_two, lambda z, xl, xh, y, c: (z, 1 - xl, 1, y, c) if (xh, c) == (0, 1) else None)
    step_three = moved(
        step_two,
        lambda z, xl, xh, y, c: (z - 1, xl, xh, y, c) if c == 0 else (z + 1, kind(xl, xh), xh, y, c),
    )
    turned_four = moved(step_three, lambda z, xl, xh, y, c: (z + 1, xl, xh, y, 1) if c == 1 else None)

    parts = numerators(late_kernel, 1, where, nvir, swap_one, swap_two, step_two)
    early, parts = lax.optimization_barrier((early, parts))
    early, late = jnp.sum(early, axis=0), jnp.sum(exchanged(parts), axis=0)

    mine_energy, one_energy, swap_energy = energy(mine), energy(step_one), energy(swap_one)
    amps_one = amps(
        early[0], jnp.where(c == 0, mine_energy, one_energy), jnp.where(c == 0, one_energy, swap_energy)
    )
    amps_zero = amps(early[1], mine_energy, jnp.where(xh == 0, mine_energy, energy(beyond)))
    first = moved(
        amps_one,
        lambda z, xl, xh, y, c: (z + 1, kind(xl, xh), xh, y, 1) if c == 0 else (z - 1, xl, xh, y, 0),
    )
    second = moved(
        amps_one,
        lambda z, xl, xh, y, c: (z + 1, kind(xl, xh), xh, y, 1) if c == 1 else None,
    )
    second = jnp.where(c == 0, amps_one, second)
    late, first, second, amps_zero, turned_one, turned_two, step_three = lax.optimization_barrier(
        (late, first, second, amps_zero, turned_one, turned_two, step_three)
    )

    first, second = by_hops(first, second)

    amps_two = amps(late[0], jnp.where(c == 0, swap_energy, energy(swap_two)), energy(step_two))
    third = moved(
        amps_two,
        lambda z, xl, xh, y, c: (z - 1, xl, xh, y, 0) if c == 0 else (z - 2, xl, xh, y, 1),
    )
    fourth = moved(amps_two, lambda z, xl, xh, y, c: (z + 2, kind(xl, xh), xh, y, 1) if c == 0 else None)
    fourth = jnp.where(c == 0, amps_zero, fourth)
    third, fourth, first, second, turned_two = lax.optimization_barrier((third, fourth, first, second, turned_two))
    third, fourth = by_hops(third, fourth)

    def product(dot, *blocks):
        return lambda parts: sum(dot(part, block[:nvir]) for part, block in zip(parts, blocks))

    case = xh * NC + c
    begun = lax.switch(
        case,
        [
            product(dot_nn, step_two, step_one),
            product(dot_tn, step_one, step_two),
            product(dot_nn, step_two, step_one),
            product(dot_tn, turned_one, turned_two),
        ],
        (first, second),
    )

    def ending(h, k, dot, *blocks):
        def branch(parts, total):
            total = total + product(dot, *blocks)(parts)
            cut = [total[:, n * depth : (n + 1) * depth] for n in range(NXH * NC)]
            sent = jnp.concatenate([cut[NC * (1 - h) + 1 - k], cut[NC * h + 1 - k]], axis=1)
            return sent, cut[NC * (1 - h) + k], cut[NC * h + k]

        return branch

    sent, theirs, ours = lax.switch(
        case,
        [
            ending(0, 0, dot_nn, step_three, mine),
            ending(0, 1, dot_tn, turned_four, step_three),
            ending(1, 0, dot_nn, step_three, beyond),
            ending(1, 1, dot_tn, turned_four, step_three),
        ],
        (third, fourth),
        begun,
    )
    got = other_core(sent)
    return (ours + got[:, depth:] + across(theirs + got[:, :depth]))[None]


def solution(mesh):
    grid = Mesh(mesh.devices.reshape(NZ, NXL, NXH, NY, NC), ALL)
    return jax.shard_map(
        local,
        mesh=grid,
        in_specs=(P(("z", "xl"), None, ("xh", "y", "c")), P(("z", "xl")), P()),
        out_specs=P(("z", "xl"), None, ("xh", "y", "c")),
        check_vma=False,
    )
```

```python
import jax
import jax.numpy as jnp
from jax import lax
from jax.experimental import pallas as pl
from jax.experimental.pallas import tpu as pltpu
from jax.sharding import Mesh, PartitionSpec as P

NZ, NXL, NXH, NY, NC = 8, 2, 2, 4, 2
ALL = ("z", "xl", "xh", "y", "c")


def flat(z, xl, xh, y, c):
    return (((z % NZ * NXL + xl % NXL) * NXH + xh % NXH) * NY + y % NY) * NC + c % NC


def moved(array, where):
    pairs = []
    for z in range(NZ):
        for xl in range(NXL):
            for xh in range(NXH):
                for y in range(NY):
                    for c in range(NC):
                        target = where(z, xl, xh, y, c)
                        if target is not None:
                            pairs.append((flat(z, xl, xh, y, c), flat(*target)))
    return lax.ppermute(array, ALL, pairs)


def other_core(array):
    return moved(array, lambda z, xl, xh, y, c: (z, xl, xh, y, 1 - c))


def across(array):
    return moved(array, lambda z, xl, xh, y, c: (z, xl, 1 - xh, y, c))


def kind(xl, xh):
    return xl if xh == 0 else 1 - xl


def dot_nt(a, b):
    return lax.dot_general(a, b, (((1,), (1,)), ((), ())), preferred_element_type=jnp.float32)


def dot_nn(a, b):
    return lax.dot_general(a, b, (((1,), (0,)), ((), ())), preferred_element_type=jnp.float32)


def dot_tn(a, b):
    return lax.dot_general(a, b, (((0,), (0,)), ((), ())), preferred_element_type=jnp.float32)


def numer_into(a_ref, b_ref, out_ref, slot):
    nvir = out_ref.shape[3]
    a, b = a_ref[:nvir, :], b_ref[:nvir, :]
    value = 2.0 * dot_nt(a, b) - dot_nt(b, a)
    out_ref[:, slot] = value.reshape(out_ref.shape[0], out_ref.shape[2], nvir)


def early_kernel(where_ref, mine_ref, one_ref, swap_ref, beyond_ref, out_ref):
    @pl.when(where_ref[0] == 0)
    def _():
        numer_into(mine_ref, one_ref, out_ref, 0)

    @pl.when(where_ref[0] != 0)
    def _():
        numer_into(one_ref, swap_ref, out_ref, 0)

    @pl.when(where_ref[1] == 0)
    def _():
        numer_into(mine_ref, mine_ref, out_ref, 1)

    @pl.when(where_ref[1] != 0)
    def _():
        numer_into(mine_ref, beyond_ref, out_ref, 1)


def late_kernel(where_ref, swap_one_ref, swap_two_ref, two_ref, out_ref):
    @pl.when(where_ref[0] == 0)
    def _():
        numer_into(swap_one_ref, two_ref, out_ref, 0)

    @pl.when(where_ref[0] != 0)
    def _():
        numer_into(swap_two_ref, two_ref, out_ref, 0)


def numerators(kernel, count, where, nvir, *blocks):
    share = nvir // NY
    width = blocks[0].shape[1]
    return pl.pallas_call(
        kernel,
        out_shape=jax.ShapeDtypeStruct((NY, count, share, nvir), jnp.float32),
        in_specs=[pl.BlockSpec(memory_space=pltpu.SMEM)] + [pl.BlockSpec(memory_space=pltpu.VMEM)] * len(blocks),
        out_specs=pl.BlockSpec(memory_space=pltpu.VMEM),
        cost_estimate=pl.CostEstimate(
            flops=4 * count * nvir * nvir * width,
            bytes_accessed=2 * len(blocks) * nvir * width + 4 * count * nvir * nvir,
            transcendentals=0,
        ),
        compiler_params=pltpu.CompilerParams(vmem_limit_bytes=24 * 2**20),
    )(where, *blocks)


def local(three_index, occ_energy, vir_energy):
    own = three_index[0]
    nvir, depth = own.shape
    share = nvir // NY
    c, xh, y = lax.axis_index("c"), lax.axis_index("xh"), lax.axis_index("y")

    high = lax.reduce_precision(occ_energy[0], 8, 7)
    rest = occ_energy[0] - high
    middle = lax.reduce_precision(rest, 8, 7)
    line = lax.broadcasted_iota(jnp.int32, (8, 4 * depth), 0)
    tail = jnp.where(line == 0, high, jnp.where(line == 1, middle, jnp.where(line == 2, rest - middle, 0.0)))
    there = across(own)
    beside = other_core(own)
    there, tail = lax.optimization_barrier((there, tail.astype(jnp.bfloat16)))
    there_beside = other_core(there)

    def in_order(first, a, b):
        return jnp.where(first, jnp.concatenate([a, b], axis=1), jnp.concatenate([b, a], axis=1))

    mine = in_order(xh == 0, in_order(c == 0, own, beside), in_order(c == 0, there, there_beside))
    mine = jnp.concatenate([mine, tail], axis=0)

    step_one = moved(
        mine,
        lambda z, xl, xh, y, c: (z - 1, kind(xl, xh), xh, y, c) if c == 0 else (z + 1, xl, xh, y, c),
    )
    beyond = moved(mine, lambda z, xl, xh, y, c: (z, 1 - xl, 1, y, c) if (xh, c) == (0, 0) else None)
    swap_one = other_core(step_one)
    step_two = moved(step_one, lambda z, xl, xh, y, c: (z - 1 if c == 0 else z + 1, xl, xh, y, c))

    def exchanged(parts):
        return lax.all_to_all(parts, "y", 0, 0, tiled=True)

    def energy(block):
        terms = block[nvir:, :nvir].astype(jnp.float32)
        return terms[0:1] + terms[1:2] + terms[2:3]

    vir_rows = lax.dynamic_slice_in_dim(vir_energy, y * share, share)
    virs = vir_rows[:, None] + vir_energy[None, :]

    def amps(value, a, b):
        return (value / (virs - a - b)).astype(jnp.bfloat16)

    def by_hops(*parts):
        parts = jnp.stack(parts)
        hops = [parts] + [moved(parts, lambda z, xl, xh, y, c, n=n: (z, xl, xh, y - n, c)) for n in range(1, NY)]
        return [
            jnp.concatenate([lax.select_n(y, *(hops[(k - n) % NY][m] for n in range(NY))) for k in range(NY)], axis=0)
            for m in range(parts.shape[0])
        ]

    where = jnp.stack([c, xh])
    parts = numerators(early_kernel, 2, where, nvir, mine, step_one, swap_one, beyond)
    parts, swap_one, step_one_after = lax.optimization_barrier((parts, swap_one, step_one))
    swap_two = moved(swap_one, lambda z, xl, xh, y, c: (z - 1, xl, xh, y, 1) if c == 1 else None)
    turned_one = moved(step_one_after, lambda z, xl, xh, y, c: (z, 1 - xl, 1, y, c) if (xh, c) == (0, 1) else None)
    early = exchanged(parts)
    turned_two = moved(step_two, lambda z, xl, xh, y, c: (z, 1 - xl, 1, y, c) if (xh, c) == (0, 1) else None)
    step_three = moved(
        step_two,
        lambda z, xl, xh, y, c: (z - 1, xl, xh, y, c) if c == 0 else (z + 1, kind(xl, xh), xh, y, c),
    )
    turned_four = moved(step_three, lambda z, xl, xh, y, c: (z + 1, xl, xh, y, 1) if c == 1 else None)

    parts = numerators(late_kernel, 1, where, nvir, swap_one, swap_two, step_two)
    early, parts = lax.optimization_barrier((early, parts))
    early, late = jnp.sum(early, axis=0), jnp.sum(exchanged(parts), axis=0)

    mine_energy, one_energy, swap_energy = energy(mine), energy(step_one), energy(swap_one)
    amps_one = amps(
        early[0], jnp.where(c == 0, mine_energy, one_energy), jnp.where(c == 0, one_energy, swap_energy)
    )
    amps_zero = amps(early[1], mine_energy, jnp.where(xh == 0, mine_energy, energy(beyond)))
    first = moved(
        amps_one,
        lambda z, xl, xh, y, c: (z + 1, kind(xl, xh), xh, y, 1) if c == 0 else (z - 1, xl, xh, y, 0),
    )
    second = moved(
        amps_one,
        lambda z, xl, xh, y, c: (z + 1, kind(xl, xh), xh, y, 1) if c == 1 else None,
    )
    second = jnp.where(c == 0, amps_one, second)
    late, first, second, amps_zero, turned_one, turned_two, step_three = lax.optimization_barrier(
        (late, first, second, amps_zero, turned_one, turned_two, step_three)
    )


    amps_two = amps(late[0], jnp.where(c == 0, swap_energy, energy(swap_two)), energy(step_two))
    third = moved(
        amps_two,
        lambda z, xl, xh, y, c: (z - 1, xl, xh, y, 0) if c == 0 else (z - 2, xl, xh, y, 1),
    )
    fourth = moved(amps_two, lambda z, xl, xh, y, c: (z + 2, kind(xl, xh), xh, y, 1) if c == 0 else None)
    fourth = jnp.where(c == 0, amps_zero, fourth)
    third, fourth, first, second, turned_two = lax.optimization_barrier((third, fourth, first, second, turned_two))
    first, second, third, fourth = by_hops(first, second, third, fourth)

    def product(dot, *blocks):
        return lambda parts: sum(dot(part, block[:nvir]) for part, block in zip(parts, blocks))

    case = xh * NC + c
    begun = lax.switch(
        case,
        [
            product(dot_nn, step_two, step_one),
            product(dot_tn, step_one, step_two),
            product(dot_nn, step_two, step_one),
            product(dot_tn, turned_one, turned_two),
        ],
        (first, second),
    )

    def ending(h, k, dot, *blocks):
        def branch(parts, total):
            total = total + product(dot, *blocks)(parts)
            cut = [total[:, n * depth : (n + 1) * depth] for n in range(NXH * NC)]
            sent = jnp.concatenate([cut[NC * (1 - h) + 1 - k], cut[NC * h + 1 - k]], axis=1)
            return sent, cut[NC * (1 - h) + k], cut[NC * h + k]

        return branch

    sent, theirs, ours = lax.switch(
        case,
        [
            ending(0, 0, dot_nn, step_three, mine),
            ending(0, 1, dot_tn, turned_four, step_three),
            ending(1, 0, dot_nn, step_three, beyond),
            ending(1, 1, dot_tn, turned_four, step_three),
        ],
        (third, fourth),
        begun,
    )
    got = other_core(sent)
    return (ours + got[:, depth:] + across(theirs + got[:, :depth]))[None]


def solution(mesh):
    grid = Mesh(mesh.devices.reshape(NZ, NXL, NXH, NY, NC), ALL)
    return jax.shard_map(
        local,
        mesh=grid,
        in_specs=(P(("z", "xl"), None, ("xh", "y", "c")), P(("z", "xl")), P()),
        out_specs=P(("z", "xl"), None, ("xh", "y", "c")),
        check_vma=False,
    )
```

```python
import jax
import jax.numpy as jnp
from jax import lax
from jax.experimental import pallas as pl
from jax.experimental.pallas import tpu as pltpu
from jax.sharding import Mesh, PartitionSpec as P

NZ, NXL, NXH, NY, NC = 8, 2, 2, 4, 2
ALL = ("z", "xl", "xh", "y", "c")


def flat(z, xl, xh, y, c):
    return (((z % NZ * NXL + xl % NXL) * NXH + xh % NXH) * NY + y % NY) * NC + c % NC


def moved(array, where):
    pairs = []
    for z in range(NZ):
        for xl in range(NXL):
            for xh in range(NXH):
                for y in range(NY):
                    for c in range(NC):
                        target = where(z, xl, xh, y, c)
                        if target is not None:
                            pairs.append((flat(z, xl, xh, y, c), flat(*target)))
    return lax.ppermute(array, ALL, pairs)


def other_core(array):
    return moved(array, lambda z, xl, xh, y, c: (z, xl, xh, y, 1 - c))


def across(array):
    return moved(array, lambda z, xl, xh, y, c: (z, xl, 1 - xh, y, c))


def kind(xl, xh):
    return xl if xh == 0 else 1 - xl


def dot_nt(a, b):
    return lax.dot_general(a, b, (((1,), (1,)), ((), ())), preferred_element_type=jnp.float32)


def dot_nn(a, b):
    return lax.dot_general(a, b, (((1,), (0,)), ((), ())), preferred_element_type=jnp.float32)


def dot_tn(a, b):
    return lax.dot_general(a, b, (((0,), (0,)), ((), ())), preferred_element_type=jnp.float32)


def numer_into(a_ref, b_ref, out_ref, slot):
    nvir = out_ref.shape[3]
    a, b = a_ref[:nvir, :], b_ref[:nvir, :]
    value = 2.0 * dot_nt(a, b) - dot_nt(b, a)
    out_ref[:, slot] = value.reshape(out_ref.shape[0], out_ref.shape[2], nvir)


def early_kernel(where_ref, mine_ref, one_ref, swap_ref, beyond_ref, out_ref):
    @pl.when(where_ref[0] == 0)
    def _():
        numer_into(mine_ref, one_ref, out_ref, 0)

    @pl.when(where_ref[0] != 0)
    def _():
        numer_into(one_ref, swap_ref, out_ref, 0)

    @pl.when(where_ref[1] == 0)
    def _():
        numer_into(mine_ref, mine_ref, out_ref, 1)

    @pl.when(where_ref[1] != 0)
    def _():
        numer_into(mine_ref, beyond_ref, out_ref, 1)


def late_kernel(where_ref, swap_one_ref, swap_two_ref, two_ref, out_ref):
    @pl.when(where_ref[0] == 0)
    def _():
        numer_into(swap_one_ref, two_ref, out_ref, 0)

    @pl.when(where_ref[0] != 0)
    def _():
        numer_into(swap_two_ref, two_ref, out_ref, 0)


def numerators(kernel, count, where, nvir, *blocks):
    share = nvir // NY
    width = blocks[0].shape[1]
    return pl.pallas_call(
        kernel,
        out_shape=jax.ShapeDtypeStruct((NY, count, share, nvir), jnp.float32),
        in_specs=[pl.BlockSpec(memory_space=pltpu.SMEM)] + [pl.BlockSpec(memory_space=pltpu.VMEM)] * len(blocks),
        out_specs=pl.BlockSpec(memory_space=pltpu.VMEM),
        cost_estimate=pl.CostEstimate(
            flops=4 * count * nvir * nvir * width,
            bytes_accessed=2 * len(blocks) * nvir * width + 4 * count * nvir * nvir,
            transcendentals=0,
        ),
        compiler_params=pltpu.CompilerParams(vmem_limit_bytes=24 * 2**20),
    )(where, *blocks)


def local(three_index, occ_energy, vir_energy):
    own = three_index[0]
    nvir, depth = own.shape
    share = nvir // NY
    c, xh, y = lax.axis_index("c"), lax.axis_index("xh"), lax.axis_index("y")

    high = lax.reduce_precision(occ_energy[0], 8, 7)
    rest = occ_energy[0] - high
    middle = lax.reduce_precision(rest, 8, 7)
    line = lax.broadcasted_iota(jnp.int32, (8, 4 * depth), 0)
    tail = jnp.where(line == 0, high, jnp.where(line == 1, middle, jnp.where(line == 2, rest - middle, 0.0)))
    there = across(own)
    beside = other_core(own)
    there, tail = lax.optimization_barrier((there, tail.astype(jnp.bfloat16)))
    there_beside = other_core(there)

    def in_order(first, a, b):
        return jnp.where(first, jnp.concatenate([a, b], axis=1), jnp.concatenate([b, a], axis=1))

    mine = in_order(xh == 0, in_order(c == 0, own, beside), in_order(c == 0, there, there_beside))
    mine = jnp.concatenate([mine, tail], axis=0)

    step_one = moved(
        mine,
        lambda z, xl, xh, y, c: (z - 1, kind(xl, xh), xh, y, c) if c == 0 else (z + 1, xl, xh, y, c),
    )
    beyond = moved(mine, lambda z, xl, xh, y, c: (z, 1 - xl, 1, y, c) if (xh, c) == (0, 0) else None)
    swap_one = other_core(step_one)
    step_two = moved(step_one, lambda z, xl, xh, y, c: (z - 1 if c == 0 else z + 1, xl, xh, y, c))

    def exchanged(parts):
        return lax.all_to_all(parts, "y", 0, 0, tiled=True)

    def energy(block):
        terms = block[nvir:, :nvir].astype(jnp.float32)
        return terms[0:1] + terms[1:2] + terms[2:3]

    vir_rows = lax.dynamic_slice_in_dim(vir_energy, y * share, share)
    virs = vir_rows[:, None] + vir_energy[None, :]

    def amps(value, a, b):
        return (value / (virs - a - b)).astype(jnp.bfloat16)

    def by_hops(*parts):
        parts = jnp.stack(parts)
        hops = [parts] + [moved(parts, lambda z, xl, xh, y, c, n=n: (z, xl, xh, y - n, c)) for n in range(1, NY)]
        return [
            jnp.concatenate([lax.select_n(y, *(hops[(k - n) % NY][m] for n in range(NY))) for k in range(NY)], axis=0)
            for m in range(parts.shape[0])
        ]

    where = jnp.stack([c, xh])
    parts = numerators(early_kernel, 2, where, nvir, mine, step_one, swap_one, beyond)
    parts, swap_one, step_one_after = lax.optimization_barrier((parts, swap_one, step_one))
    swap_two = moved(swap_one, lambda z, xl, xh, y, c: (z - 1, xl, xh, y, 1) if c == 1 else None)
    turned_one = moved(step_one_after, lambda z, xl, xh, y, c: (z, 1 - xl, 1, y, c) if (xh, c) == (0, 1) else None)
    early = exchanged(parts)
    turned_two = moved(step_two, lambda z, xl, xh, y, c: (z, 1 - xl, 1, y, c) if (xh, c) == (0, 1) else None)
    step_three = moved(
        step_two,
        lambda z, xl, xh, y, c: (z - 1, xl, xh, y, c) if c == 0 else (z + 1, kind(xl, xh), xh, y, c),
    )
    turned_four = moved(step_three, lambda z, xl, xh, y, c: (z + 1, xl, xh, y, 1) if c == 1 else None)

    parts = numerators(late_kernel, 1, where, nvir, swap_one, swap_two, step_two)
    early, parts = lax.optimization_barrier((early, parts))
    early, late = jnp.sum(early, axis=0), jnp.sum(exchanged(parts), axis=0)

    mine_energy, one_energy, swap_energy = energy(mine), energy(step_one), energy(swap_one)
    amps_one = amps(
        early[0], jnp.where(c == 0, mine_energy, one_energy), jnp.where(c == 0, one_energy, swap_energy)
    )
    amps_zero = amps(early[1], mine_energy, jnp.where(xh == 0, mine_energy, energy(beyond)))
    first = moved(
        amps_one,
        lambda z, xl, xh, y, c: (z + 1, kind(xl, xh), xh, y, 1) if c == 0 else (z - 1, xl, xh, y, 0),
    )
    second = moved(
        amps_one,
        lambda z, xl, xh, y, c: (z + 1, kind(xl, xh), xh, y, 1) if c == 1 else None,
    )
    second = jnp.where(c == 0, amps_one, second)
    late, first, second, amps_zero = lax.optimization_barrier((late, first, second, amps_zero))

    first, second = by_hops(first, second)

    amps_two = amps(late[0], jnp.where(c == 0, swap_energy, energy(swap_two)), energy(step_two))
    third = moved(
        amps_two,
        lambda z, xl, xh, y, c: (z - 1, xl, xh, y, 0) if c == 0 else (z - 2, xl, xh, y, 1),
    )
    fourth = moved(amps_two, lambda z, xl, xh, y, c: (z + 2, kind(xl, xh), xh, y, 1) if c == 0 else None)
    fourth = jnp.where(c == 0, amps_zero, fourth)
    third, fourth, first, second, turned_two = lax.optimization_barrier((third, fourth, first, second, turned_two))
    third, fourth = by_hops(third, fourth)

    def product(dot, *blocks):
        return lambda parts: sum(dot(part, block[:nvir]) for part, block in zip(parts, blocks))

    case = xh * NC + c
    begun = lax.switch(
        case,
        [
            product(dot_nn, step_two, step_one),
            product(dot_tn, step_one, step_two),
            product(dot_nn, step_two, step_one),
            product(dot_tn, turned_one, turned_two),
        ],
        (first, second),
    )

    def ending(h, k, dot, *blocks):
        def branch(parts, total):
            total = total + product(dot, *blocks)(parts)
            cut = [total[:, n * depth : (n + 1) * depth] for n in range(NXH * NC)]
            sent = jnp.concatenate([cut[NC * (1 - h) + 1 - k], cut[NC * h + 1 - k]], axis=1)
            return sent, cut[NC * (1 - h) + k], cut[NC * h + k]

        return branch

    sent, theirs, ours = lax.switch(
        case,
        [
            ending(0, 0, dot_nn, step_three, mine),
            ending(0, 1, dot_tn, turned_four, step_three),
            ending(1, 0, dot_nn, step_three, beyond),
            ending(1, 1, dot_tn, turned_four, step_three),
        ],
        (third, fourth),
        begun,
    )
    got = other_core(sent)
    return (ours + got[:, depth:] + across(theirs + got[:, :depth]))[None]


def solution(mesh):
    grid = Mesh(mesh.devices.reshape(NZ, NXL, NXH, NY, NC), ALL)
    return jax.shard_map(
        local,
        mesh=grid,
        in_specs=(P(("z", "xl"), None, ("xh", "y", "c")), P(("z", "xl")), P()),
        out_specs=P(("z", "xl"), None, ("xh", "y", "c")),
        check_vma=False,
    )
```
